256 devices in a mesh: vocab: 32 (over x, z), prange: 4 (over y), query: 2 (over core).
Axes of the slice: x: 4, y: 4, z: 8, core: 2. Of those that a mesh axis runs over, the one named last changes fastest.
Arguments:
- term_ids: int32 [4096, 32], P('query'), may hold values from 0 to 32767
- term_weights: bfloat16 [4096, 32], P('query'), may hold values from 0.049804688 to 1
- impact: bfloat16 [32768, 8192], P('vocab', 'prange'), may hold values from 0.0099487305 to 1
- query_rows: bfloat16 [128, 32768], P(('prange', 'query'), 'vocab'), may hold values from -0.3125 to 0.3125
- candidates: int32 [128, 4], P(('prange', 'query')), may hold values from 0 to 63, all different within a row; in each aligned block of 16 rows (0 to 15, 16 to 31, ...) at most 2 rows name the same one
Outputs:
- first_scores: bfloat16 [4, 2048, 4096], P('prange', 'vocab', 'query')
- rescored: float32 [128, 4, 128], P(('prange', 'query'), None, 'vocab')
The draws below stay inside these ranges and needn't reach their ends.
Inputs may be any that keep to these rules, and one draw needn't show every extreme that they name: `candidates`: each row names 4 different blocks. The 16 rows held by one device name any block at most 2 times, and some block exactly 2 times.
All inputs are finite; a program needn't handle non-finite values.
Results may differ from the reference program's by a relative error of at most 0.019.
Values may be sent and summed in bfloat16 or wider, within the bound.
No kernel may reach another device: no remote copies, remote signals or barrier semaphores. Data moves between devices by JAX's collectives and lax.ppermute only.
A program may use at most 64 MiB of HBM per device.

```python
import math
import jax
import jax.numpy as jnp
import numpy as np
from jax import lax

VOCAB = 32768
TERMS = 32
PRUNED = 4096
BLOCK = 128
BLOCKS = 64
PASSAGES = 8192
FULL_ROWS_LOCAL = 16
ROWS = 128
CANDS = 4
MOST = 2
N_VOCAB = 32
N_PRANGE = 4


def plant(result, own_key, low, largest):
    extent = result.shape
    spot = [jax.random.randint(jax.random.fold_in(own_key, axis), (), 0, extent[axis]) for axis in range(len(extent))]
    result = result.at[tuple(spot)].set(low)
    longest = extent.index(max(extent))
    spot[longest] = (spot[longest] + 1) % extent[longest]
    return result.at[tuple(spot)].set(largest)


def block_levels(own_key, shape, split, low, top_value):
    def one(position, shards_of):
        draws = jax.random.uniform(jax.random.fold_in(jax.random.fold_in(own_key, 6), position), (shards_of,), jnp.float32, low / len(split), top_value / len(split))
        return jnp.repeat(jnp.exp(draws), shape[position] // shards_of).reshape((-1,) + (1,) * (len(shape) - position - 1))

    loudness = one(*split[0])
    for cut in split[1:]:
        loudness = loudness * one(*cut)
    return loudness


def cumulative_ranks(number_of, skew):
    loads = [(1 << 20) // math.isqrt(grade ** skew) + 1 for grade in range(1, number_of + 1)]
    scale = 1 + sum(loads) // (1 << 30)
    return np.cumsum(np.array([max(1, weight // scale) for weight in loads]))


def skewed_ids(own_key, extent, count, slope):
    listing = cumulative_ranks(count, slope)
    lot = jax.random.randint(jax.random.fold_in(own_key, 1), extent, 0, int(listing[count - 1]))
    grade = jnp.searchsorted(jnp.asarray(listing, jnp.int32), lot, side="right")
    return jax.random.permutation(jax.random.fold_in(own_key, 2), count)[grade].astype(jnp.int32)


def assign_block(key, own, number, rows, amount, top, most, lean):
    order = jax.random.permutation(key, amount)
    packed, usual = load_shares(amount, rows * top, most, lean, True), load_shares(amount, rows * top, most, lean, False)
    places = jnp.arange(amount)

    def named(sizes, turn):
        used = int((sizes > 0).sum())
        fixed = max(1, used // 4)
        moved = fixed + (places - fixed + turn * (used - fixed)) % max(1, amount - fixed)
        return jnp.zeros((amount,), jnp.int32).at[order[jnp.where(places < fixed, places, moved)]].set(jnp.asarray(sizes, jnp.int32))

    sizes = jnp.where(number % 4 == 0, named(packed, number // 4), named(usual, number - number // 4 - 1))
    mixed = jax.random.permutation(jax.random.fold_in(own, 3), amount)
    donor, taker = mixed[0:amount // 2 * 2:2], mixed[1:amount // 2 * 2:2]
    margin = jnp.minimum(sizes[donor] - 1, most - sizes[taker]) // 2
    margin = jnp.where((donor == order[0]) | (taker == order[0]) | (sizes[taker] == 0), 0, jnp.maximum(margin, 0))
    moved = jax.random.randint(jax.random.fold_in(own, 4), (amount // 2,), 0, 1 << 20) % (margin + 1)
    sizes = sizes.at[donor].add(-moved).at[taker].add(moved)
    items = jnp.searchsorted(jnp.cumsum(sizes), jnp.arange(rows * top), side="right").astype(jnp.int32)
    listing = items.reshape(top, rows).T
    listing = listing[jax.random.permutation(jax.random.fold_in(own, 1), rows)]
    turn = jax.random.randint(jax.random.fold_in(own, 2), (rows, 1), 0, top)
    return jnp.take_along_axis(listing, (jnp.arange(top)[None, :] + turn) % top, axis=1)


def load_shares(amount, total, limit, lean, full):
    weights = [(1 << 20) // math.isqrt(standing ** lean) + 1 for standing in range(1, amount + 1)]
    largest = limit if full else min(limit, max(-(-total // amount), total * weights[0] // sum(weights)))
    least = 1 if total - largest >= amount - 1 else 0
    counts, rest = [largest] + [least] * (amount - 1), total - largest - least * (amount - 1)
    while rest > 0:
        free = [i for i in range(1, amount) if counts[i] < largest] or [i for i in range(1, amount) if counts[i] < limit]
        pool, budget = sum([weights[i] for i in free]), rest
        for i in free:
            extra = min(limit - counts[i], max(1, budget * weights[i] // pool), rest)
            counts[i] = counts[i] + extra
            rest = rest - extra
    return np.array(counts)


def scatter_about(key, shape, scale, most, pieces=(), kind=jnp.bfloat16):
    array = jax.random.normal(key, shape, jnp.float32) * scale
    if len(pieces) > 0:
        array = block_levels(key, shape, pieces, -0.22, 0.18) * array
    return jnp.clip(array, min=-most, max=most).astype(kind)


def setup_inputs(seed: int = 0) -> dict:
    arg_keys = jax.random.split(jax.random.key(seed), 6)
    term_ids = plant(skewed_ids(arg_keys[0], (PRUNED, TERMS), VOCAB, 2), jax.random.fold_in(arg_keys[0], 3), 0, VOCAB - 1).astype(jnp.int32)
    term_weights = jnp.clip(jnp.exp(math.log(1.0) - 2.9996462 * jax.random.uniform(arg_keys[1], (PRUNED, TERMS), jnp.float32) ** block_levels(arg_keys[1], (PRUNED, TERMS), ((0, 2),), -0.2, 0.2)), 0.049804688, 1.0).astype(jnp.bfloat16)
    impact = jnp.clip(jnp.exp(math.log(1.0) - 4.61031033 * jax.random.uniform(arg_keys[2], (VOCAB, PASSAGES), jnp.float32) ** block_levels(arg_keys[2], (VOCAB, PASSAGES), ((0, 32), (1, 4)), -0.2, 0.2)), 0.0099487305, 1.0).astype(jnp.bfloat16)
    query_rows = scatter_about(arg_keys[3], (ROWS, VOCAB), 0.02, 0.3125, ((0, 8), (1, 32)))
    candidates_keys = jax.random.split(jax.random.fold_in(arg_keys[4], 1), ROWS // FULL_ROWS_LOCAL)
    candidates_turns = jax.random.permutation(jax.random.fold_in(arg_keys[4], 3), ROWS // FULL_ROWS_LOCAL)
    candidates = jax.vmap(lambda own, number: assign_block(jax.random.fold_in(arg_keys[4], 2), own, number, FULL_ROWS_LOCAL, BLOCKS, CANDS, MOST, 2))(candidates_keys, candidates_turns).reshape((ROWS, CANDS))
    return dict(term_ids=term_ids, term_weights=term_weights, impact=impact, query_rows=query_rows, candidates=candidates)


def first_block(block_ids, block_weights, impact):
    same_term = (block_ids[:, :, None] == block_ids[:, None, :]).astype(jnp.float32)
    summed = jnp.einsum("qkj,qj->qk", same_term, block_weights.astype(jnp.float32), precision=lax.Precision.HIGHEST)
    merged = summed.astype(jnp.bfloat16).astype(jnp.float32) / jnp.sum(same_term, axis=2)
    collected_tiles = impact[block_ids].astype(jnp.float32)
    shard_width = VOCAB // N_VOCAB
    owners = ((block_ids // shard_width)[:, :, None] == jnp.arange(N_VOCAB, dtype=jnp.int32)[None, None, :]).astype(jnp.float32)
    weighted_impacts = merged[:, :, None] * owners
    shard_pieces = jnp.einsum("ljh,ljg->hlg", weighted_impacts, collected_tiles, precision=lax.Precision.HIGHEST)
    return jnp.sum(shard_pieces.astype(jnp.bfloat16).astype(jnp.float32), axis=0).astype(jnp.bfloat16)


def reference(term_ids, term_weights, impact, query_rows, candidates):
    block_rows = math.gcd(64, PRUNED)
    ids_blocks = term_ids.reshape(-1, block_rows, TERMS)
    weight_blocks = term_weights.reshape(-1, block_rows, TERMS)
    scores = lax.map(lambda pair: first_block(pair[0], pair[1], impact), (ids_blocks, weight_blocks))
    first_scores = scores.reshape(PRUNED, PASSAGES).T.reshape(N_PRANGE, PASSAGES // N_PRANGE, PRUNED)
    block_tiles = impact.reshape(VOCAB, BLOCKS, BLOCK)

    def one_query(pair):
        query_weight_row, blocks_row = pair
        picked = block_tiles[:, blocks_row, :].astype(jnp.float32)
        return jnp.einsum("v,vcp->cp", query_weight_row.astype(jnp.float32), picked, precision=lax.Precision.HIGHEST)

    rescored = lax.map(one_query, (query_rows, candidates))
    return (first_scores, rescored)
```

```python
import functools

import jax
import jax.numpy as jnp
from jax import lax
from jax.experimental import pallas as pl
from jax.experimental.pallas import tpu as pltpu
from jax.sharding import Mesh
from jax.sharding import PartitionSpec as P


BLOCK = 128
CANDS = 4
NX = 4
NZ = 8
NY = 4
LANES = 128
GROUP = 8
FIRST = 256
CHUNKS = 2
UNROLL = 8
F32 = jnp.float32
BF16 = jnp.bfloat16


def shifted(array, axis, shift):
    size = lax.axis_size(axis)
    return lax.ppermute(array, axis, [(i, (i + shift) % size) for i in range(size)])


def kept_in_hbm(array):
    return pltpu.with_memory_space_constraint(array, pltpu.HBM)


def dense_kernel(pos_ref, ids_ref, weights_ref, dense_ref, low_ref, key_ref):
    x, z, core = pos_ref[0], pos_ref[1], pos_ref[2]
    groups, pairs = ids_ref.shape
    highs = dense_ref.shape[1] // FIRST
    ids = ids_ref[...]
    low_ref[...] = (ids & (FIRST - 1)).astype(F32)
    x_rel = ((ids >> 13) - x) & (NX - 1)
    half_rel = ((ids >> 9) & 1) ^ core
    high = x_rel * 4 + half_rel * 2 + ((ids >> 8) & 1)
    lane = lax.broadcasted_iota(jnp.int32, ids.shape, 1)
    key = high * GROUP + lane // (pairs // GROUP)
    key_ref[...] = jnp.where(((ids >> 10) & (NZ - 1)) == z, key, -1).astype(F32)
    low_rows = lax.broadcasted_iota(jnp.int32, (FIRST, pairs), 0).astype(F32).astype(BF16)
    key_rows = lax.broadcasted_iota(jnp.int32, (highs * GROUP, pairs), 0).astype(F32).astype(BF16)
    one = jnp.ones((), BF16)
    zero = jnp.zeros((), BF16)

    def one_group(g):
        low = low_ref[pl.ds(g, 1), :].astype(BF16)
        keys = key_ref[pl.ds(g, 1), :].astype(BF16)
        weights = weights_ref[pl.ds(g, 1), :].astype(BF16)
        ones = jnp.where(low_rows == low, one, zero)
        spread = jnp.where(key_rows == keys, weights, zero)
        made = lax.dot_general(spread, ones, (((1,), (1,)), ((), ())), preferred_element_type=F32)
        return made.reshape(highs, GROUP, FIRST)

    def pair_of_groups(i, carry):
        both = jnp.concatenate([one_group(2 * i), one_group(2 * i + 1)], axis=1).astype(BF16)
        row = pl.multiple_of(i * 2 * GROUP, 2 * GROUP)
        for h in range(highs):
            dense_ref[pl.ds(row, 2 * GROUP), h * FIRST : (h + 1) * FIRST] = both[h]
        return carry

    lax.fori_loop(0, groups // 2, pair_of_groups, 0, unroll=UNROLL)


def build_dense(place, ids, weights, width, chunk):
    blocks = 4
    pairs = ids.shape[1]
    groups = ids.shape[0] // CHUNKS // blocks
    queries = groups * GROUP
    spec = pl.BlockSpec((groups, pairs), lambda i, s: (chunk * blocks + i, 0))
    return pl.pallas_call(
        dense_kernel,
        out_shape=pltpu.HBM((queries * blocks, width), BF16),
        grid_spec=pltpu.PrefetchScalarGridSpec(
            num_scalar_prefetch=1,
            grid=(blocks,),
            in_specs=[spec, spec],
            out_specs=pl.BlockSpec((queries, width), lambda i, s: (i, 0)),
            scratch_shapes=[pltpu.VMEM((groups, pairs), F32), pltpu.VMEM((groups, pairs), F32)],
        ),
        compiler_params=pltpu.CompilerParams(vmem_limit_bytes=8 << 20),
        cost_estimate=pl.CostEstimate(flops=10**10, transcendentals=0, bytes_accessed=queries * blocks * width * 2),
        name="dense_build",
    )(place, ids, weights)


def rows_kernel(pos_ref, r0, r1, r2, r3, impact_ref, o0, o1, o2, o3):
    y = pos_ref[3]
    step = pl.program_id(0)
    width = impact_ref.shape[0]
    full = r0.shape[0]
    rows = jnp.concatenate([r[:, :width] for r in (r0, r1, r2, r3)], axis=0)
    scores = jnp.dot(rows, impact_ref[...], preferred_element_type=F32)
    blocks = impact_ref.shape[1] // BLOCK
    here = (y * pl.num_programs(0) + step) * blocks

    @pl.when(step == 0)
    def _():
        for o in (o0, o1, o2, o3):
            o[...] = jnp.zeros_like(o)

    for home, (r, o) in enumerate(((r0, o0), (r1, o1), (r2, o2), (r3, o3))):
        named = r[:, width : width + LANES].astype(F32).astype(jnp.int32) - here
        mine = scores[home * full : (home + 1) * full]
        for c in range(CANDS):
            column = named[:, c : c + 1]
            picked = o[c * full : (c + 1) * full, :].astype(F32)
            for b in range(blocks):
                picked = jnp.where(column == b, mine[:, b * BLOCK : (b + 1) * BLOCK], picked)
            o[c * full : (c + 1) * full, :] = picked.astype(BF16)


def score_rows(place, gathered, impact):
    steps = 4
    full, wide = gathered[0].shape
    width, passages = impact.shape
    one = jax.ShapeDtypeStruct((full * CANDS, BLOCK), BF16)
    rows = pl.BlockSpec((full, wide), lambda i, s: (0, 0), pipeline_mode=pl.Buffered(1))
    return pl.pallas_call(
        rows_kernel,
        out_shape=[one] * NY,
        grid_spec=pltpu.PrefetchScalarGridSpec(
            num_scalar_prefetch=1,
            grid=(steps,),
            in_specs=[rows] * NY + [pl.BlockSpec((width, passages // steps), lambda i, s: (0, i))],
            out_specs=[pl.BlockSpec((full * CANDS, BLOCK), lambda i, s: (0, 0))] * NY,
        ),
        compiler_params=pltpu.CompilerParams(vmem_limit_bytes=8 << 20),
        cost_estimate=pl.CostEstimate(flops=2 * 10**9, transcendentals=0, bytes_accessed=4 << 20),
        name="score_rows",
    )(place, *gathered, kept_in_hbm(impact))


def score_kernel(pos_ref, dense_ref, *refs, extra):
    piece_refs = refs[:8]
    extra_refs = refs[8:12] if extra else ()
    out_refs = refs[-NZ - 1 : -1]
    made_ref = refs[-1]
    x, z = pos_ref[0], pos_ref[1]
    rows, width = dense_ref.shape[1:]
    depth = piece_refs[0].shape[0]
    chunk = made_ref.shape[1]
    half = LANES // 2
    step = pl.program_id(0)
    last = step == pl.num_programs(0) - 1
    total = None
    for i, piece in enumerate(piece_refs):
        block = dense_ref[:, :, i * depth : (i + 1) * depth].reshape(2 * rows, depth)
        one = jnp.dot(block, piece[...], preferred_element_type=F32)
        total = one if total is None else total + one
    left = lax.broadcasted_iota(jnp.int32, (rows, LANES), 1) < half
    at = pl.ds(pl.multiple_of(step * rows, rows), rows)
    for m in range(NZ // 2):
        a = total[:rows, m * LANES : (m + 1) * LANES]
        b = total[rows:, m * LANES : (m + 1) * LANES]
        made_ref[2 * m, at, :] = jnp.where(left, a, pltpu.roll(b, half, 1)).astype(BF16)
        made_ref[2 * m + 1, at, :] = jnp.where(left, pltpu.roll(a, half, 1), b).astype(BF16)

    @pl.when(last)
    def _():
        for j, out_ref in enumerate(out_refs):
            out_ref[:chunk, :] = made_ref[(z + j) & (NZ - 1)]
        if extra:
            pack_rows(x, chunk, extra_refs, out_refs)


def pack_rows(x, chunk, extra_refs, out_refs):
    total = extra_refs[0][...].astype(F32)
    for r in extra_refs[1:]:
        total = total + r[...].astype(F32)
    share = LANES // NX
    total = pltpu.roll(total, (LANES - x * share) & (LANES - 1), 1)
    full = total.shape[0] // CANDS
    lane = lax.broadcasted_iota(jnp.int32, (full, LANES), 1) // share
    packed = jnp.zeros((full, LANES), F32)
    for c in range(CANDS):
        part = total[c * full : (c + 1) * full]
        if c:
            part = pltpu.roll(part, c * share, 1)
        packed = jnp.where(lane == c, part, packed)
    packed = packed.astype(BF16)
    for out_ref in out_refs:
        out_ref[chunk:, :] = packed


def score_chunk(place, dense, pieces, sums):
    steps = 4
    chunk = dense.shape[0] // 2
    width = dense.shape[1]
    share = pieces[0].shape[1]
    extra = sums is not None
    out_rows = chunk + (sums[0].shape[0] // CANDS if extra else 0)
    more = tuple(sums) if extra else ()
    vmem = pl.BlockSpec(memory_space=pltpu.VMEM)
    return pl.pallas_call(
        functools.partial(score_kernel, extra=extra),
        out_shape=[jax.ShapeDtypeStruct((out_rows, LANES), BF16)] * NZ,
        grid_spec=pltpu.PrefetchScalarGridSpec(
            num_scalar_prefetch=1,
            grid=(steps,),
            in_specs=[pl.BlockSpec((2, chunk // steps, width), lambda i, s: (0, i, 0))]
            + [vmem] * (len(pieces) + len(more)),
            out_specs=[vmem] * NZ,
            scratch_shapes=[pltpu.VMEM((NZ, chunk, LANES), BF16)],
        ),
        compiler_params=pltpu.CompilerParams(vmem_limit_bytes=16 << 20),
        cost_estimate=pl.CostEstimate(
            flops=2 * chunk * width * share * 2, transcendentals=0, bytes_accessed=chunk * width * 4
        ),
        name="score_chunk",
    )(place, kept_in_hbm(dense.reshape(2, chunk, width)), *pieces, *more)


def cut_kernel(pos_ref, impact_ref, *refs, shifts):
    out_refs, sem = refs[:-1], refs[-1]
    x, core = pos_ref[0], pos_ref[2]
    copies = []
    for i, (out_ref, r) in enumerate(zip(out_refs, shifts)):
        depth, share = out_ref.shape
        to_x = (x - r) & (NX - 1)
        at = (pl.ds(core * depth, depth), pl.ds(to_x * share, share))
        copies.append(pltpu.make_async_copy(impact_ref.at[at], out_ref, sem.at[i]))
    for copy in copies:
        copy.start()
    for copy in copies:
        copy.wait()


def cut_slices(place, impact, shifts):
    one = jax.ShapeDtypeStruct((impact.shape[0] // 2, impact.shape[1] // NX), BF16)
    return pl.pallas_call(
        functools.partial(cut_kernel, shifts=shifts),
        out_shape=[one] * len(shifts),
        in_specs=[pl.BlockSpec(memory_space=pltpu.SMEM), pl.BlockSpec(memory_space=pltpu.HBM)],
        out_specs=[pl.BlockSpec(memory_space=pltpu.VMEM)] * len(shifts),
        scratch_shapes=[pltpu.SemaphoreType.DMA((len(shifts),))],
        compiler_params=pltpu.CompilerParams(vmem_limit_bytes=4 << 20),
        name="cut_slices",
    )(place, kept_in_hbm(impact))


def final_kernel(pos_ref, a0, a1, a2, b0, b1, b2, first_ref, rescored_ref):
    z = pos_ref[1]
    half = LANES // 2
    chunk = a1.shape[0]
    column = 0
    for own, one, two in ((a0, a1, a2), (b0, b1, b2)):
        total = own[:chunk].astype(F32) + one[:chunk].astype(F32) + two[:chunk].astype(F32)
        turned = total.T.astype(BF16)
        first_ref[:, column : column + chunk] = turned[:half]
        first_ref[:, column + chunk : column + 2 * chunk] = turned[half:]
        column += 2 * chunk
    more = b0[chunk:].astype(F32) + b1[chunk:].astype(F32) + b2[chunk:].astype(F32)
    share = LANES // (NX * NZ)
    turned = pltpu.roll(more, (LANES - z * share) & (LANES - 1), 1).T
    wide = LANES // CANDS
    for c in range(CANDS):
        rescored_ref[c] = turned[c * wide : c * wide + share]


def finish(place, parts, full):
    chunk = parts[1].shape[0]
    vmem = pl.BlockSpec(memory_space=pltpu.VMEM)
    return pl.pallas_call(
        final_kernel,
        out_shape=[
            jax.ShapeDtypeStruct((LANES // 2, 4 * chunk), BF16),
            jax.ShapeDtypeStruct((CANDS, LANES // (NX * NZ), full), F32),
        ],
        in_specs=[pl.BlockSpec(memory_space=pltpu.SMEM)] + [vmem] * 6,
        out_specs=[vmem] * 2,
        compiler_params=pltpu.CompilerParams(vmem_limit_bytes=8 << 20),
        name="finish",
    )(place, *parts)


def added(*parts):
    total = parts[0].astype(F32)
    for part in parts[1:]:
        total = total + part.astype(F32)
    return total.astype(BF16)


def ring(made, long_right):
    right = [4, 3, 2, 1] if long_right else [3, 2, 1]
    left = [5, 6, 7]
    flows = {1: right, -1: left}
    carried = {}
    ahead = None
    for step in range(4):
        for way, slots in flows.items():
            if step < len(slots):
                value = made[slots[step]]
                if step:
                    if step == 1 and way == -1 and ahead is not None:
                        value = added(carried[way], value, ahead)
                    else:
                        value = added(carried[way], value)
                elif way == -1 and not long_right:
                    ahead = shifted(made[4], "z", -2)
                carried[way] = shifted(value, "z", way)
    return carried[1], carried[-1]


def local(term_ids, term_weights, impact, query_rows, candidates):
    x = lax.axis_index("x")
    z = lax.axis_index("z")
    y = lax.axis_index("prange")
    core = lax.axis_index("query")
    place = jnp.stack([x, z, core, y]).astype(jnp.int32)
    shard_width, passages = impact.shape
    queries, terms = term_ids.shape
    full = query_rows.shape[0]
    pair_lanes = GROUP * terms
    half_terms = shard_width // 2
    share = passages // NX

    def cut(whole, half, to_x):
        return lax.dynamic_slice(whole, (half * half_terms, to_x * share), (half_terms, share))

    def after(values, done):
        return lax.optimization_barrier((values, done))[0]

    shifts = (1, 3, 2)
    sent = dict(zip(shifts, cut_slices(place, impact, shifts)))
    near = {r: shifted(sent[r], "x", -r) for r in shifts}
    (term_ids, term_weights), sent = lax.optimization_barrier(((term_ids, term_weights), sent))

    ids = term_ids.reshape(queries // GROUP, pair_lanes)
    weights = term_weights.astype(F32).reshape(queries // GROUP, pair_lanes)
    dense_a = build_dense(place, ids, weights, NX * shard_width, 0)

    query_rows, candidates, impact = after((query_rows, candidates, impact), dense_a)
    named = jnp.pad(candidates.astype(BF16), ((0, 0), (0, LANES - CANDS)))
    rows = jnp.concatenate([query_rows, named], axis=1)
    gathered = [rows] + [shifted(rows, "prange", -r) for r in (1, 2, 3)]
    ids, rows = lax.optimization_barrier((ids, rows))
    dense_b = build_dense(place, ids, weights, NX * shard_width, 1)
    gathered = after(gathered, dense_b)
    by_home = score_rows(place, gathered, impact)
    back = [by_home[0]] + [shifted(by_home[r], "prange", r) for r in (1, 2, 3)]

    impact, near = after((impact, near), by_home)
    pieces = [cut(impact, core, x), cut(impact, 1 - core, x)]
    for r in (1, 2, 3):
        pieces += [near[r], shifted(near[r], "query", 1)]

    made_a = score_chunk(place, dense_a, pieces, None)
    a1, a2 = ring(made_a, True)
    back = after(back, made_a)
    mine = added(*back)
    sums = [mine] + [shifted(mine, "x", r) for r in (1, 2, 3)]
    made_b = score_chunk(place, dense_b, pieces, sums)
    b1, b2 = ring(made_b, False)
    first, rescored = finish(place, (made_a[0], a1, a2, made_b[0], b1, b2), full)
    return (first[None], jnp.transpose(rescored, (2, 0, 1)))


def solution(mesh):
    finer = Mesh(
        mesh.devices.reshape(NX, NZ, mesh.shape["prange"], mesh.shape["query"]),
        ("x", "z", "prange", "query"),
    )
    vocab = ("x", "z")
    in_specs = (
        P("query", None),
        P("query", None),
        P(vocab, "prange"),
        P(("prange", "query"), vocab),
        P(("prange", "query"), None),
    )
    out_specs = (P("prange", vocab, "query"), P(("prange", "query"), None, vocab))
    return jax.shard_map(local, mesh=finer, in_specs=in_specs, out_specs=out_specs, check_vma=False)
```

```python
import functools

import jax
import jax.numpy as jnp
from jax import lax
from jax.experimental import pallas as pl
from jax.experimental.pallas import tpu as pltpu
from jax.sharding import Mesh
from jax.sharding import PartitionSpec as P


BLOCK = 128
CANDS = 4
NX = 4
NZ = 8
NY = 4
LANES = 128
GROUP = 8
FIRST = 256
CHUNKS = 2
UNROLL = 8
CUTS = 4
F32 = jnp.float32
BF16 = jnp.bfloat16


def shifted(array, axis, shift):
    size = lax.axis_size(axis)
    return lax.ppermute(array, axis, [(i, (i + shift) % size) for i in range(size)])


def kept_in_hbm(array):
    return pltpu.with_memory_space_constraint(array, pltpu.HBM)


def dense_kernel(pos_ref, ids_ref, weights_ref, dense_ref, turned_ref, low_ref, key_ref, weight_ref):
    x, z, core = pos_ref[0], pos_ref[1], pos_ref[2]
    terms, queries = ids_ref.shape
    groups, pairs = low_ref.shape
    highs = dense_ref.shape[1] // FIRST
    ids = ids_ref[...]
    x_rel = ((ids >> 13) - x) & (NX - 1)
    half_rel = ((ids >> 9) & 1) ^ core
    high = x_rel * 4 + half_rel * 2 + ((ids >> 8) & 1)
    key = high * GROUP + (lax.broadcasted_iota(jnp.int32, ids.shape, 1) & (GROUP - 1))
    key = jnp.where(((ids >> 10) & (NZ - 1)) == z, key, -1)
    low = (ids & (FIRST - 1)).astype(F32)
    weights = weights_ref[...].astype(F32)
    turned_ref[...] = jnp.concatenate([low, key.astype(F32), weights, weights], axis=0).T
    place = lax.broadcasted_iota(jnp.int32, (groups, LANES), 1) // terms
    across = LANES // terms
    for kind, to_ref in enumerate((low_ref, key_ref, weight_ref)):
        for side in range(pairs // LANES):
            row = None
            for j in range(across):
                part = turned_ref[pl.ds(side * across + j, groups, stride=GROUP), :]
                shift = (terms * (j - kind)) % LANES
                part = pltpu.roll(part, shift, 1) if shift else part
                row = part if row is None else jnp.where(place == j, part, row)
            to_ref[:, side * LANES : (side + 1) * LANES] = row
    low_rows = lax.broadcasted_iota(jnp.int32, (FIRST, pairs), 0).astype(F32).astype(BF16)
    key_rows = lax.broadcasted_iota(jnp.int32, (highs * GROUP, pairs), 0).astype(F32).astype(BF16)
    one = jnp.ones((), BF16)
    zero = jnp.zeros((), BF16)

    def one_group(g):
        low = low_ref[pl.ds(g, 1), :].astype(BF16)
        keys = key_ref[pl.ds(g, 1), :].astype(BF16)
        weights = weight_ref[pl.ds(g, 1), :].astype(BF16)
        ones = jnp.where(low_rows == low, one, zero)
        spread = jnp.where(key_rows == keys, weights, zero)
        made = lax.dot_general(spread, ones, (((1,), (1,)), ((), ())), preferred_element_type=F32)
        return made.reshape(highs, GROUP, FIRST)

    def pair_of_groups(i, carry):
        both = jnp.concatenate([one_group(2 * i), one_group(2 * i + 1)], axis=1).astype(BF16)
        row = pl.multiple_of(i * 2 * GROUP, 2 * GROUP)
        for h in range(highs):
            dense_ref[pl.ds(row, 2 * GROUP), h * FIRST : (h + 1) * FIRST] = both[h]
        return carry

    lax.fori_loop(0, groups // 2, pair_of_groups, 0, unroll=UNROLL)


def build_dense(place, ids, weights, width, chunk):
    blocks = 2
    terms = ids.shape[0]
    queries = ids.shape[1] // CHUNKS // blocks
    groups = queries // GROUP
    spec = pl.BlockSpec((terms, queries), lambda i, s: (0, chunk * blocks + i))
    rows = pltpu.VMEM((groups, GROUP * terms), F32)
    return pl.pallas_call(
        dense_kernel,
        out_shape=pltpu.HBM((queries * blocks, width), BF16),
        grid_spec=pltpu.PrefetchScalarGridSpec(
            num_scalar_prefetch=1,
            grid=(blocks,),
            in_specs=[spec, spec],
            out_specs=pl.BlockSpec((queries, width), lambda i, s: (i, 0)),
            scratch_shapes=[pltpu.VMEM((queries, LANES), F32), rows, rows, rows],
        ),
        compiler_params=pltpu.CompilerParams(vmem_limit_bytes=12 << 20),
        cost_estimate=pl.CostEstimate(flops=10**10, transcendentals=0, bytes_accessed=queries * blocks * width * 2),
        name="dense_build",
    )(place, ids, weights)


def rows_kernel(pos_ref, r0, r1, r2, r3, impact_ref, o0, o1, o2, o3):
    y = pos_ref[3]
    width = impact_ref.shape[0]
    full = r0.shape[0]
    rows = jnp.concatenate([r[:, :width] for r in (r0, r1, r2, r3)], axis=0)
    scores = jnp.dot(rows, impact_ref[...], preferred_element_type=F32)
    blocks = impact_ref.shape[1] // BLOCK
    for home, (r, o) in enumerate(((r0, o0), (r1, o1), (r2, o2), (r3, o3))):
        named = r[:, width : width + LANES].astype(F32).astype(jnp.int32) - y * blocks
        mine = scores[home * full : (home + 1) * full]
        for c in range(CANDS):
            column = named[:, c : c + 1]
            picked = jnp.zeros((full, BLOCK), F32)
            for b in range(blocks):
                picked = jnp.where(column == b, mine[:, b * BLOCK : (b + 1) * BLOCK], picked)
            o[c * full : (c + 1) * full, :] = picked.astype(BF16)


def score_rows(place, gathered, impact):
    full = gathered[0].shape[0]
    one = jax.ShapeDtypeStruct((full * CANDS, BLOCK), BF16)
    vmem = pl.BlockSpec(memory_space=pltpu.VMEM)
    return pl.pallas_call(
        rows_kernel,
        out_shape=[one] * NY,
        in_specs=[pl.BlockSpec(memory_space=pltpu.SMEM)] + [vmem] * 5,
        out_specs=[vmem] * NY,
        compiler_params=pltpu.CompilerParams(vmem_limit_bytes=8 << 20),
        cost_estimate=pl.CostEstimate(flops=2 * 10**9, transcendentals=0, bytes_accessed=4 << 20),
        name="score_rows",
    )(place, *gathered, impact)


def score_kernel(pos_ref, dense_ref, *refs, extra):
    piece_refs = refs[:8]
    extra_refs = refs[8:12] if extra else ()
    out_refs = refs[-NZ - 1 : -1]
    made_ref = refs[-1]
    x, z = pos_ref[0], pos_ref[1]
    rows, width = dense_ref.shape[1:]
    depth = piece_refs[0].shape[0]
    chunk = made_ref.shape[1]
    half = LANES // 2
    step = pl.program_id(0)
    last = step == pl.num_programs(0) - 1
    made = []
    for part in range(2):
        total = None
        for i, piece in enumerate(piece_refs):
            block = dense_ref[part, :, i * depth : (i + 1) * depth]
            one = jnp.dot(block, piece[...], preferred_element_type=F32)
            total = one if total is None else total + one
        made.append(total)
    left = lax.broadcasted_iota(jnp.int32, (rows, LANES), 1) < half
    at = pl.ds(pl.multiple_of(step * rows, rows), rows)
    for m in range(NZ // 2):
        a = made[0][:, m * LANES : (m + 1) * LANES]
        b = made[1][:, m * LANES : (m + 1) * LANES]
        made_ref[2 * m, at, :] = jnp.where(left, a, pltpu.roll(b, half, 1)).astype(BF16)
        made_ref[2 * m + 1, at, :] = jnp.where(left, pltpu.roll(a, half, 1), b).astype(BF16)

    @pl.when(last)
    def _():
        for j, out_ref in enumerate(out_refs):
            out_ref[:chunk, :] = made_ref[(z + j) & (NZ - 1)]
        if extra:
            pack_rows(x, chunk, extra_refs, out_refs)


def pack_rows(x, chunk, extra_refs, out_refs):
    total = extra_refs[0][...].astype(F32)
    for r in extra_refs[1:]:
        total = total + r[...].astype(F32)
    share = LANES // NX
    total = pltpu.roll(total, (LANES - x * share) & (LANES - 1), 1)
    full = total.shape[0] // CANDS
    lane = lax.broadcasted_iota(jnp.int32, (full, LANES), 1) // share
    packed = jnp.zeros((full, LANES), F32)
    for c in range(CANDS):
        part = total[c * full : (c + 1) * full]
        if c:
            part = pltpu.roll(part, c * share, 1)
        packed = jnp.where(lane == c, part, packed)
    packed = packed.astype(BF16)
    for out_ref in out_refs:
        out_ref[chunk:, :] = packed


def score_chunk(place, dense, pieces, sums):
    steps = 2
    chunk = dense.shape[0] // 2
    width = dense.shape[1]
    share = pieces[0].shape[1]
    extra = sums is not None
    out_rows = chunk + (sums[0].shape[0] // CANDS if extra else 0)
    more = tuple(sums) if extra else ()
    halves = dense.reshape(2, chunk, width)
    vmem = pl.BlockSpec(memory_space=pltpu.VMEM)
    return pl.pallas_call(
        functools.partial(score_kernel, extra=extra),
        out_shape=[jax.ShapeDtypeStruct((out_rows, LANES), BF16)] * NZ,
        grid_spec=pltpu.PrefetchScalarGridSpec(
            num_scalar_prefetch=1,
            grid=(steps,),
            in_specs=[pl.BlockSpec((2, chunk // steps, width), lambda i, s: (0, i, 0))]
            + [vmem] * (len(pieces) + len(more)),
            out_specs=[vmem] * NZ,
            scratch_shapes=[pltpu.VMEM((NZ, chunk, LANES), BF16)],
        ),
        compiler_params=pltpu.CompilerParams(vmem_limit_bytes=20 << 20),
        cost_estimate=pl.CostEstimate(
            flops=2 * chunk * width * share * 2, transcendentals=0, bytes_accessed=chunk * width * 4
        ),
        name="score_chunk",
    )(place, kept_in_hbm(halves) if not extra else halves, *pieces, *more)


def cut_kernel(pos_ref, impact_ref, query_ref, named_ref, *refs, shifts):
    rows_ref, out_refs, sem = refs[0], refs[1:-1], refs[-1]
    x, core = pos_ref[0], pos_ref[2]
    copies = []
    for i, (out_ref, r) in enumerate(zip(out_refs, shifts)):
        depth, share = out_ref.shape
        part = depth // CUTS
        to_x = (x - r) & (NX - 1)
        for j in range(CUTS):
            at = (pl.ds(core * depth + j * part, part), pl.ds(to_x * share, share))
            copies.append(
                pltpu.make_async_copy(impact_ref.at[at], out_ref.at[pl.ds(j * part, part)], sem.at[i * CUTS + j])
            )
    for copy in copies:
        copy.start()
    full, width = query_ref.shape
    rows_ref[:, :width] = query_ref[...]
    named = named_ref[...].astype(F32)
    named = jnp.concatenate([named, jnp.zeros((LANES - CANDS, full), F32)], axis=0)
    rows_ref[:, width:] = named.T.astype(BF16)
    for copy in copies:
        copy.wait()


def cut_slices(place, impact, query_rows, candidates, shifts):
    full, width = query_rows.shape
    one = jax.ShapeDtypeStruct((impact.shape[0] // 2, impact.shape[1] // NX), BF16)
    vmem = pl.BlockSpec(memory_space=pltpu.VMEM)
    rows, *cuts = pl.pallas_call(
        functools.partial(cut_kernel, shifts=shifts),
        out_shape=[jax.ShapeDtypeStruct((full, width + LANES), BF16)] + [one] * len(shifts),
        in_specs=[pl.BlockSpec(memory_space=pltpu.SMEM), pl.BlockSpec(memory_space=pltpu.HBM), vmem, vmem],
        out_specs=[vmem] * (1 + len(shifts)),
        scratch_shapes=[pltpu.SemaphoreType.DMA((len(shifts) * CUTS,))],
        compiler_params=pltpu.CompilerParams(vmem_limit_bytes=4 << 20),
        name="cut_slices",
    )(place, kept_in_hbm(impact), query_rows, candidates.T)
    return rows, cuts


def final_kernel(pos_ref, a0, a1, a2, b0, b1, b2, first_ref, rescored_ref):
    z = pos_ref[1]
    half = LANES // 2
    chunk = a1.shape[0]
    column = 0
    for own, one, two in ((a0, a1, a2), (b0, b1, b2)):
        total = own[:chunk].astype(F32) + one[:chunk].astype(F32) + two[:chunk].astype(F32)
        turned = total.T.astype(BF16)
        first_ref[:, column : column + chunk] = turned[:half]
        first_ref[:, column + chunk : column + 2 * chunk] = turned[half:]
        column += 2 * chunk
    more = b0[chunk:].astype(F32) + b1[chunk:].astype(F32) + b2[chunk:].astype(F32)
    share = LANES // (NX * NZ)
    turned = pltpu.roll(more, (LANES - z * share) & (LANES - 1), 1).T
    wide = LANES // CANDS
    for c in range(CANDS):
        rescored_ref[c] = turned[c * wide : c * wide + share]


def finish(place, parts, full):
    chunk = parts[1].shape[0]
    vmem = pl.BlockSpec(memory_space=pltpu.VMEM)
    return pl.pallas_call(
        final_kernel,
        out_shape=[
            jax.ShapeDtypeStruct((LANES // 2, 4 * chunk), BF16),
            jax.ShapeDtypeStruct((CANDS, LANES // (NX * NZ), full), F32),
        ],
        in_specs=[pl.BlockSpec(memory_space=pltpu.SMEM)] + [vmem] * 6,
        out_specs=[vmem] * 2,
        compiler_params=pltpu.CompilerParams(vmem_limit_bytes=8 << 20),
        name="finish",
    )(place, *parts)


def added(*parts):
    total = parts[0].astype(F32)
    for part in parts[1:]:
        total = total + part.astype(F32)
    return total.astype(BF16)


def ring(made, long_way):
    flows = {1: [3, 2, 1], -1: [5, 6, 7]}
    carried = {}
    ahead = None
    for step in range(3):
        for way, slots in flows.items():
            value = made[slots[step]]
            if step == 1 and way == long_way:
                value = added(carried[way], value, ahead)
            elif step:
                value = added(carried[way], value)
            elif way == long_way:
                ahead = shifted(made[4], "z", 2 * way)
            carried[way] = shifted(value, "z", way)
    return carried[1], carried[-1]


def local(term_ids, term_weights, impact, query_rows, candidates):
    x = lax.axis_index("x")
    z = lax.axis_index("z")
    y = lax.axis_index("prange")
    core = lax.axis_index("query")
    place = jnp.stack([x, z, core, y]).astype(jnp.int32)
    shard_width, passages = impact.shape
    full = query_rows.shape[0]
    half_terms = shard_width // 2
    share = passages // NX

    def cut(whole, half, to_x):
        return lax.dynamic_slice(whole, (half * half_terms, to_x * share), (half_terms, share))

    def after(values, done):
        return lax.optimization_barrier((values, done))[0]

    shifts = (1, 3, 2)
    rows, cuts = cut_slices(place, impact, query_rows, candidates, shifts)
    near = {r: shifted(one, "x", -r) for r, one in zip(shifts, cuts)}
    (term_ids, term_weights), rows = lax.optimization_barrier(((term_ids, term_weights), rows))
    gathered = [rows] + [shifted(rows, "prange", -r) for r in (1, 2, 3)]

    ids = term_ids.T
    weights = term_weights.T
    dense_a = build_dense(place, ids, weights, NX * shard_width, 0)
    gathered = after(gathered, dense_a)
    by_home = score_rows(place, gathered, impact)
    back = [by_home[0]] + [shifted(by_home[r], "prange", r) for r in (1, 2, 3)]
    ids = after(ids, by_home)
    dense_b = build_dense(place, ids, weights, NX * shard_width, 1)

    impact, near, back = after((impact, near, back), dense_b)
    pieces = [cut(impact, core, x), cut(impact, 1 - core, x)]
    for r in (1, 2, 3):
        pieces += [near[r], shifted(near[r], "query", 1)]
    mine = added(*back)
    sums = [mine] + [shifted(mine, "x", r) for r in (1, 2, 3)]

    made_a = score_chunk(place, dense_a, pieces, None)
    a1, a2 = ring(made_a, 1)
    made_b = score_chunk(place, dense_b, pieces, sums)
    b1, b2 = ring(made_b, -1)
    first, rescored = finish(place, (made_a[0], a1, a2, made_b[0], b1, b2), full)
    return (first[None], jnp.transpose(rescored, (2, 0, 1)))


def solution(mesh):
    finer = Mesh(
        mesh.devices.reshape(NX, NZ, mesh.shape["prange"], mesh.shape["query"]),
        ("x", "z", "prange", "query"),
    )
    vocab = ("x", "z")
    in_specs = (
        P("query", None),
        P("query", None),
        P(vocab, "prange"),
        P(("prange", "query"), vocab),
        P(("prange", "query"), None),
    )
    out_specs = (P("prange", vocab, "query"), P(("prange", "query"), None, vocab))
    return jax.shard_map(local, mesh=finer, in_specs=in_specs, out_specs=out_specs, check_vma=False)
```

```python
import functools

import jax
import jax.numpy as jnp
from jax import lax
from jax.experimental import pallas as pl
from jax.experimental.pallas import tpu as pltpu
from jax.sharding import Mesh
from jax.sharding import PartitionSpec as P


BLOCK = 128
CANDS = 4
NX = 4
NZ = 8
NY = 4
LANES = 128
GROUP = 8
FIRST = 256
CHUNKS = 2
UNROLL = 32
CUTS = 4
F32 = jnp.float32
BF16 = jnp.bfloat16


def shifted(array, axis, shift):
    size = lax.axis_size(axis)
    return lax.ppermute(array, axis, [(i, (i + shift) % size) for i in range(size)])


def kept_in_hbm(array):
    return pltpu.with_memory_space_constraint(array, pltpu.HBM)


def dense_kernel(pos_ref, ids_ref, weights_ref, dense_ref, turned_ref, low_ref, key_ref, weight_ref):
    x, z, core = pos_ref[0], pos_ref[1], pos_ref[2]
    terms, _ = ids_ref.shape
    groups, pairs = low_ref.shape
    highs = dense_ref.shape[1] // FIRST
    ids = ids_ref[...]
    x_rel = ((ids >> 13) - x) & (NX - 1)
    half_rel = ((ids >> 9) & 1) ^ core
    high = x_rel * 4 + half_rel * 2 + ((ids >> 8) & 1)
    key = high * GROUP + (lax.broadcasted_iota(jnp.int32, ids.shape, 1) & (GROUP - 1))
    key = jnp.where(((ids >> 10) & (NZ - 1)) == z, key, -1)
    low = (ids & (FIRST - 1)).astype(F32)
    weights = weights_ref[...].astype(F32)
    turned_ref[...] = jnp.concatenate([low, key.astype(F32), weights, weights], axis=0).T
    place = lax.broadcasted_iota(jnp.int32, (groups, LANES), 1) // terms
    across = LANES // terms
    for kind, to_ref in enumerate((low_ref, key_ref, weight_ref)):
        for side in range(pairs // LANES):
            row = None
            for j in range(across):
                part = turned_ref[pl.ds(side * across + j, groups, stride=GROUP), :]
                shift = (terms * (j - kind)) % LANES
                part = pltpu.roll(part, shift, 1) if shift else part
                row = part if row is None else jnp.where(place == j, part, row)
            to_ref[:, side * LANES : (side + 1) * LANES] = row
    low_rows = lax.broadcasted_iota(jnp.int32, (FIRST, pairs), 0).astype(F32).astype(BF16)
    key_rows = lax.broadcasted_iota(jnp.int32, (highs * GROUP, pairs), 0).astype(F32).astype(BF16)
    one = jnp.ones((), BF16)
    zero = jnp.zeros((), BF16)

    def one_group(g):
        low = low_ref[pl.ds(g, 1), :].astype(BF16)
        keys = key_ref[pl.ds(g, 1), :].astype(BF16)
        weights = weight_ref[pl.ds(g, 1), :].astype(BF16)
        ones = jnp.where(low_rows == low, one, zero)
        spread = jnp.where(key_rows == keys, weights, zero)
        made = lax.dot_general(spread, ones, (((1,), (1,)), ((), ())), preferred_element_type=F32)
        return made.reshape(highs, GROUP, FIRST)

    def pair_of_groups(i, carry):
        both = jnp.concatenate([one_group(2 * i), one_group(2 * i + 1)], axis=1).astype(BF16)
        row = pl.multiple_of(i * 2 * GROUP, 2 * GROUP)
        for h in range(highs):
            dense_ref[pl.ds(row, 2 * GROUP), h * FIRST : (h + 1) * FIRST] = both[h]
        return carry

    lax.fori_loop(0, groups // 2, pair_of_groups, 0, unroll=UNROLL)


def build_dense(place, ids, weights, width, chunk):
    blocks = 2
    terms = ids.shape[0]
    queries = ids.shape[1] // CHUNKS // blocks
    groups = queries // GROUP
    spec = pl.BlockSpec((terms, queries), lambda i, s: (0, chunk * blocks + i))
    rows = pltpu.VMEM((groups, GROUP * terms), F32)
    return pl.pallas_call(
        dense_kernel,
        out_shape=pltpu.HBM((queries * blocks, width), BF16),
        grid_spec=pltpu.PrefetchScalarGridSpec(
            num_scalar_prefetch=1,
            grid=(blocks,),
            in_specs=[spec, spec],
            out_specs=pl.BlockSpec((queries, width), lambda i, s: (i, 0)),
            scratch_shapes=[pltpu.VMEM((queries, LANES), F32), rows, rows, rows],
        ),
        compiler_params=pltpu.CompilerParams(vmem_limit_bytes=12 << 20),
        cost_estimate=pl.CostEstimate(flops=10**10, transcendentals=0, bytes_accessed=queries * blocks * width * 2),
        name="dense_build",
    )(place, kept_in_hbm(ids), kept_in_hbm(weights))


def rows_kernel(pos_ref, r0, r1, r2, r3, impact_ref, o0, o1, o2, o3):
    y = pos_ref[3]
    width = impact_ref.shape[0]
    full = r0.shape[0]
    rows = jnp.concatenate([r[:, :width] for r in (r0, r1, r2, r3)], axis=0)
    scores = jnp.dot(rows, impact_ref[...], preferred_element_type=F32)
    blocks = impact_ref.shape[1] // BLOCK
    for home, (r, o) in enumerate(((r0, o0), (r1, o1), (r2, o2), (r3, o3))):
        named = r[:, width : width + LANES].astype(F32).astype(jnp.int32) - y * blocks
        mine = scores[home * full : (home + 1) * full]
        for c in range(CANDS):
            column = named[:, c : c + 1]
            picked = jnp.zeros((full, BLOCK), F32)
            for b in range(blocks):
                picked = jnp.where(column == b, mine[:, b * BLOCK : (b + 1) * BLOCK], picked)
            o[c * full : (c + 1) * full, :] = picked.astype(BF16)


def score_rows(place, gathered, impact):
    full = gathered[0].shape[0]
    one = jax.ShapeDtypeStruct((full * CANDS, BLOCK), BF16)
    vmem = pl.BlockSpec(memory_space=pltpu.VMEM)
    return pl.pallas_call(
        rows_kernel,
        out_shape=[one] * NY,
        in_specs=[pl.BlockSpec(memory_space=pltpu.SMEM)] + [vmem] * 5,
        out_specs=[vmem] * NY,
        compiler_params=pltpu.CompilerParams(vmem_limit_bytes=8 << 20),
        cost_estimate=pl.CostEstimate(flops=2 * 10**9, transcendentals=0, bytes_accessed=4 << 20),
        name="score_rows",
    )(place, *gathered, impact)


def score_kernel(pos_ref, dense_ref, *refs, extra):
    piece_refs = refs[:8]
    extra_refs = refs[8:12] if extra else ()
    out_refs = refs[-NZ - 1 : -1]
    made_ref = refs[-1]
    z = pos_ref[1]
    rows, _ = dense_ref.shape[1:]
    depth = piece_refs[0].shape[0]
    chunk = made_ref.shape[1]
    half = LANES // 2
    step = pl.program_id(0)
    last = step == pl.num_programs(0) - 1
    made = []
    for part in range(2):
        total = None
        for i, piece in enumerate(piece_refs):
            block = dense_ref[part, :, i * depth : (i + 1) * depth]
            one = jnp.dot(block, piece[...], preferred_element_type=F32)
            total = one if total is None else total + one
        made.append(total)
    left = lax.broadcasted_iota(jnp.int32, (rows, LANES), 1) < half
    at = pl.ds(pl.multiple_of(step * rows, rows), rows)
    for m in range(NZ // 2):
        a = made[0][:, m * LANES : (m + 1) * LANES]
        b = made[1][:, m * LANES : (m + 1) * LANES]
        made_ref[2 * m, at, :] = jnp.where(left, a, pltpu.roll(b, half, 1)).astype(BF16)
        made_ref[2 * m + 1, at, :] = jnp.where(left, pltpu.roll(a, half, 1), b).astype(BF16)

    @pl.when(last)
    def _():
        for j, out_ref in enumerate(out_refs):
            out_ref[:chunk, :] = made_ref[(z + j) & (NZ - 1)]
        if extra:
            pack_rows(z, chunk, extra_refs, out_refs)


def pack_rows(z, chunk, extra_refs, out_refs):
    total = extra_refs[0][...].astype(F32)
    for r in extra_refs[1:]:
        total = total + r[...].astype(F32)
    wide, own = LANES // NX, LANES // (NX * NZ)
    deep = total.shape[0] // NZ
    place = (lax.broadcasted_iota(jnp.int32, (deep, LANES), 1) & (wide - 1)) // own
    for j, out_ref in enumerate(out_refs):
        to_z = (z + j) & (NZ - 1)
        packed = jnp.zeros((deep, LANES), F32)
        for g in range(NZ):
            part = total[g * deep : (g + 1) * deep]
            part = pltpu.roll(part, ((g - to_z) * own) & (LANES - 1), 1)
            packed = jnp.where(place == g, part, packed)
        out_ref[chunk:, :] = jnp.concatenate([packed, jnp.zeros_like(packed)], axis=0).astype(BF16)


def score_chunk(place, dense, pieces, sums):
    steps = 2
    chunk = dense.shape[0] // 2
    width = dense.shape[1]
    share = pieces[0].shape[1]
    extra = sums is not None
    out_rows = chunk + (2 * sums[0].shape[0] // NZ if extra else 0)
    more = tuple(sums) if extra else ()
    halves = dense.reshape(2, chunk, width)
    vmem = pl.BlockSpec(memory_space=pltpu.VMEM)
    return pl.pallas_call(
        functools.partial(score_kernel, extra=extra),
        out_shape=[jax.ShapeDtypeStruct((out_rows, LANES), BF16)] * NZ,
        grid_spec=pltpu.PrefetchScalarGridSpec(
            num_scalar_prefetch=1,
            grid=(steps,),
            in_specs=[pl.BlockSpec((2, chunk // steps, width), lambda i, s: (0, i, 0))]
            + [vmem] * (len(pieces) + len(more)),
            out_specs=[vmem] * NZ,
            scratch_shapes=[pltpu.VMEM((NZ, chunk, LANES), BF16)],
        ),
        compiler_params=pltpu.CompilerParams(vmem_limit_bytes=20 << 20),
        cost_estimate=pl.CostEstimate(
            flops=2 * chunk * width * share * 2, transcendentals=0, bytes_accessed=chunk * width * 4
        ),
        name="score_chunk",
    )(place, kept_in_hbm(halves), *pieces, *more)


def cut_kernel(pos_ref, impact_ref, query_ref, named_ref, *refs, shifts):
    rows_ref, out_refs, named_here, sem = refs[0], refs[1:-2], refs[-2], refs[-1]
    x, core = pos_ref[0], pos_ref[2]
    full, width = query_ref.shape
    count = len(out_refs) * CUTS
    copies = [
        pltpu.make_async_copy(named_ref, named_here, sem.at[count]),
        pltpu.make_async_copy(query_ref, rows_ref.at[:, pl.ds(0, width)], sem.at[count + 1]),
    ]
    for i, (out_ref, r) in enumerate(zip(out_refs, shifts)):
        depth, share = out_ref.shape
        part = depth // CUTS
        to_x = (x - r) & (NX - 1)
        for j in range(CUTS):
            at = (pl.ds(core * depth + j * part, part), pl.ds(to_x * share, share))
            copies.append(
                pltpu.make_async_copy(impact_ref.at[at], out_ref.at[pl.ds(j * part, part)], sem.at[i * CUTS + j])
            )
    for copy in copies:
        copy.start()
    copies[0].wait()
    named = named_here[...].astype(F32)
    named = jnp.concatenate([named, jnp.zeros((LANES - CANDS, full), F32)], axis=0)
    rows_ref[:, width:] = named.T.astype(BF16)
    for copy in copies[1:]:
        copy.wait()


def cut_slices(place, impact, query_rows, candidates, shifts):
    full, width = query_rows.shape
    one = jax.ShapeDtypeStruct((impact.shape[0] // 2, impact.shape[1] // NX), BF16)
    vmem = pl.BlockSpec(memory_space=pltpu.VMEM)
    hbm = pl.BlockSpec(memory_space=pltpu.HBM)
    rows, *cuts = pl.pallas_call(
        functools.partial(cut_kernel, shifts=shifts),
        out_shape=[jax.ShapeDtypeStruct((full, width + LANES), BF16)] + [one] * len(shifts),
        in_specs=[pl.BlockSpec(memory_space=pltpu.SMEM), hbm, hbm, hbm],
        out_specs=[vmem] * (1 + len(shifts)),
        scratch_shapes=[
            pltpu.VMEM((CANDS, full), jnp.int32),
            pltpu.SemaphoreType.DMA((len(shifts) * CUTS + 2,)),
        ],
        compiler_params=pltpu.CompilerParams(vmem_limit_bytes=4 << 20),
        name="cut_slices",
    )(place, kept_in_hbm(impact), kept_in_hbm(query_rows), kept_in_hbm(candidates.T))
    return rows, cuts


def final_kernel(pos_ref, a0, a1, a2, b0, b1, b2, v0, v1, v2, v3, first_ref, rescored_ref):
    x = pos_ref[0]
    half = LANES // 2
    chunk = b0.shape[0]
    column = 0
    for own, one, two in ((a0, a1, a2), (b0, b1, b2)):
        total = own[:chunk].astype(F32) + one[:chunk].astype(F32) + two[:chunk].astype(F32)
        turned = total.T.astype(BF16)
        first_ref[:, column : column + chunk] = turned[:half]
        first_ref[:, column + chunk : column + 2 * chunk] = turned[half:]
        column += 2 * chunk
    more = v0[...].astype(F32) + v1[...].astype(F32) + v2[...].astype(F32) + v3[...].astype(F32)
    share = LANES // (NX * NZ)
    deep = more.shape[0] // 2
    turned = pltpu.roll(more, (LANES - x * (LANES // NX)) & (LANES - 1), 1).T
    for g in range(NZ):
        part = turned[g * share : (g + 1) * share, :deep]
        rescored_ref[g // 2, :, (g % 2) * deep : (g % 2 + 1) * deep] = part


def finish(place, parts, sums, full):
    chunk = parts[3].shape[0]
    vmem = pl.BlockSpec(memory_space=pltpu.VMEM)
    return pl.pallas_call(
        final_kernel,
        out_shape=[
            jax.ShapeDtypeStruct((LANES // 2, 4 * chunk), BF16),
            jax.ShapeDtypeStruct((CANDS, LANES // (NX * NZ), full), F32),
        ],
        in_specs=[pl.BlockSpec(memory_space=pltpu.SMEM)] + [vmem] * 10,
        out_specs=[vmem] * 2,
        compiler_params=pltpu.CompilerParams(vmem_limit_bytes=8 << 20),
        name="finish",
    )(place, *parts, *sums)


def added(*parts):
    total = parts[0].astype(F32)
    for part in parts[1:]:
        total = total + part.astype(F32)
    return total.astype(BF16)


def after(values, done):
    return lax.optimization_barrier((values, done))[0]


def sent(values):
    out = {}
    for way in (1, -1):
        out[way] = shifted(values[way], "z", way)
    return out


def first_step(made, long_way):
    ahead = shifted(made[4], "z", 2 * long_way)
    return ahead, sent({1: made[3], -1: made[5]})


def second_values(made, long_way, ahead, carried):
    values = {1: [carried[1], made[2]], -1: [carried[-1], made[6]]}
    values[long_way].append(ahead)
    return {way: added(*parts) for way, parts in values.items()}


def third_values(made, carried):
    return {1: added(carried[1], made[1]), -1: added(carried[-1], made[7])}


def rings(made_a, made_b, start_a, start_b):
    (ahead_a, going_a), (ahead_b, going_b) = start_a, start_b
    going_a = sent(second_values(made_a, 1, ahead_a, going_a))
    going_b = sent(second_values(made_b, -1, ahead_b, going_b))
    going_a = sent(third_values(made_a, going_a))
    going_b = sent(third_values(made_b, going_b))
    return (going_a[1], going_a[-1]), (going_b[1], going_b[-1])


def scored(term_ids, term_weights, impact, query_rows, candidates):
    x = lax.axis_index("x")
    z = lax.axis_index("z")
    y = lax.axis_index("prange")
    core = lax.axis_index("query")
    place = jnp.stack([x, z, core, y]).astype(jnp.int32)
    shard_width, passages = impact.shape
    full = query_rows.shape[0]
    half_terms = shard_width // 2
    share = passages // NX

    def cut(whole, half, to_x):
        return lax.dynamic_slice(whole, (half * half_terms, to_x * share), (half_terms, share))

    shifts = (1, 3, 2)
    rows, cuts = cut_slices(place, impact, query_rows, candidates, shifts)
    near = {r: shifted(one, "x", -r) for r, one in zip(shifts, cuts)}
    (term_ids, term_weights), rows = lax.optimization_barrier(((term_ids, term_weights), rows))
    gathered = [rows] + [shifted(rows, "prange", -r) for r in (1, 2, 3)]

    ids = term_ids.T
    weights = term_weights.T
    dense_a = build_dense(place, ids, weights, NX * shard_width, 0)
    gathered = after(gathered, dense_a)
    by_home = score_rows(place, gathered, impact)
    back = [by_home[0]] + [shifted(by_home[r], "prange", r) for r in (1, 2, 3)]
    ids = after(ids, by_home)
    dense_b = build_dense(place, ids, weights, NX * shard_width, 1)

    impact, near, back = after((impact, near, back), dense_b)
    pieces = [cut(impact, core, x), cut(impact, 1 - core, x)]
    for r in (1, 2, 3):
        pieces += [near[r], shifted(near[r], "query", 1)]
    made_a = score_chunk(place, dense_a, pieces, back)
    start_a = first_step(made_a, 1)
    made_b = score_chunk(place, dense_b, pieces, None)
    start_b = first_step(made_b, -1)
    (a1, a2), (b1, b2) = rings(made_a, made_b, start_a, start_b)
    chunk = made_b[0].shape[0]
    mine = added(made_a[0][chunk:], a1[chunk:], a2[chunk:])
    sums = [mine]
    for r in (1, 2, 3):
        sums.append(shifted(mine, "x", r))
    first, rescored = finish(place, (made_a[0], a1, a2, made_b[0], b1, b2), sums, full)
    return (first[None], jnp.transpose(rescored, (2, 0, 1)))


def solution(mesh):
    finer = Mesh(
        mesh.devices.reshape(NX, NZ, mesh.shape["prange"], mesh.shape["query"]),
        ("x", "z", "prange", "query"),
    )
    vocab = ("x", "z")
    in_specs = (
        P("query", None),
        P("query", None),
        P(vocab, "prange"),
        P(("prange", "query"), vocab),
        P(("prange", "query"), None),
    )
    out_specs = (P("prange", vocab, "query"), P(("prange", "query"), None, vocab))
    return jax.shard_map(scored, mesh=finer, in_specs=in_specs, out_specs=out_specs, check_vma=False)
```

```python
import functools

import jax
import jax.numpy as jnp
from jax import lax
from jax.experimental import pallas as pl
from jax.experimental.pallas import tpu as pltpu
from jax.sharding import Mesh
from jax.sharding import PartitionSpec as P


BLOCK = 128
CANDS = 4
NX = 4
NZ = 8
NY = 4
LANES = 128
GROUP = 8
FIRST = 256
CHUNKS = 2
UNROLL = 32
CUTS = 4
F32 = jnp.float32
BF16 = jnp.bfloat16


def shifted(array, axis, shift):
    size = lax.axis_size(axis)
    return lax.ppermute(array, axis, [(i, (i + shift) % size) for i in range(size)])


def kept_in_hbm(array):
    return pltpu.with_memory_space_constraint(array, pltpu.HBM)


def dense_kernel(pos_ref, ids_ref, weights_ref, dense_ref, turned_ref, low_ref, key_ref, weight_ref):
    x, z, core = pos_ref[0], pos_ref[1], pos_ref[2]
    terms, _ = ids_ref.shape
    groups, pairs = low_ref.shape
    highs = dense_ref.shape[1] // FIRST
    ids = ids_ref[...]
    x_rel = ((ids >> 13) - x) & (NX - 1)
    half_rel = ((ids >> 9) & 1) ^ core
    high = x_rel * 4 + half_rel * 2 + ((ids >> 8) & 1)
    key = high * GROUP + (lax.broadcasted_iota(jnp.int32, ids.shape, 1) & (GROUP - 1))
    key = jnp.where(((ids >> 10) & (NZ - 1)) == z, key, -1)
    low = (ids & (FIRST - 1)).astype(F32)
    weights = weights_ref[...].astype(F32)
    turned_ref[...] = jnp.concatenate([low, key.astype(F32), weights, weights], axis=0).T
    place = lax.broadcasted_iota(jnp.int32, (groups, LANES), 1) // terms
    across = LANES // terms
    for kind, to_ref in enumerate((low_ref, key_ref, weight_ref)):
        for side in range(pairs // LANES):
            row = None
            for j in range(across):
                part = turned_ref[pl.ds(side * across + j, groups, stride=GROUP), :]
                shift = (terms * (j - kind)) % LANES
                part = pltpu.roll(part, shift, 1) if shift else part
                row = part if row is None else jnp.where(place == j, part, row)
            to_ref[:, side * LANES : (side + 1) * LANES] = row
    low_rows = lax.broadcasted_iota(jnp.int32, (FIRST, pairs), 0).astype(F32).astype(BF16)
    key_rows = lax.broadcasted_iota(jnp.int32, (highs * GROUP, pairs), 0).astype(F32).astype(BF16)
    one = jnp.ones((), BF16)
    zero = jnp.zeros((), BF16)

    def one_group(g):
        low = low_ref[pl.ds(g, 1), :].astype(BF16)
        keys = key_ref[pl.ds(g, 1), :].astype(BF16)
        weights = weight_ref[pl.ds(g, 1), :].astype(BF16)
        ones = jnp.where(low_rows == low, one, zero)
        spread = jnp.where(key_rows == keys, weights, zero)
        made = lax.dot_general(spread, ones, (((1,), (1,)), ((), ())), preferred_element_type=F32)
        return made.reshape(highs, GROUP, FIRST)

    def pair_of_groups(i, carry):
        both = jnp.concatenate([one_group(2 * i), one_group(2 * i + 1)], axis=1).astype(BF16)
        row = pl.multiple_of(i * 2 * GROUP, 2 * GROUP)
        for h in range(highs):
            dense_ref[pl.ds(row, 2 * GROUP), h * FIRST : (h + 1) * FIRST] = both[h]
        return carry

    lax.fori_loop(0, groups // 2, pair_of_groups, 0, unroll=UNROLL)


def build_dense(place, ids, weights, width):
    terms, queries = ids.shape
    groups = queries // GROUP
    rows = pltpu.VMEM((groups, GROUP * terms), F32)
    vmem = pl.BlockSpec(memory_space=pltpu.VMEM)
    return pl.pallas_call(
        dense_kernel,
        out_shape=pltpu.VMEM((queries, width), BF16),
        in_specs=[pl.BlockSpec(memory_space=pltpu.SMEM), vmem, vmem],
        out_specs=vmem,
        scratch_shapes=[pltpu.VMEM((queries, LANES), F32), rows, rows, rows],
        compiler_params=pltpu.CompilerParams(vmem_limit_bytes=6 << 20),
        cost_estimate=pl.CostEstimate(flops=10**10, transcendentals=0, bytes_accessed=queries * width * 2),
        name="dense_build",
    )(place, ids, weights)


def rows_kernel(pos_ref, r0, r1, r2, r3, impact_ref, o0, o1, o2, o3):
    y = pos_ref[3]
    width = impact_ref.shape[0]
    full = r0.shape[0]
    rows = jnp.concatenate([r[:, :width] for r in (r0, r1, r2, r3)], axis=0)
    scores = jnp.dot(rows, impact_ref[...], preferred_element_type=F32)
    blocks = impact_ref.shape[1] // BLOCK
    for home, (r, o) in enumerate(((r0, o0), (r1, o1), (r2, o2), (r3, o3))):
        named = r[:, width : width + LANES].astype(F32).astype(jnp.int32) - y * blocks
        mine = scores[home * full : (home + 1) * full]
        for c in range(CANDS):
            column = named[:, c : c + 1]
            picked = jnp.zeros((full, BLOCK), F32)
            for b in range(blocks):
                picked = jnp.where(column == b, mine[:, b * BLOCK : (b + 1) * BLOCK], picked)
            o[c * full : (c + 1) * full, :] = picked.astype(BF16)


def score_rows(place, gathered, impact):
    full = gathered[0].shape[0]
    one = jax.ShapeDtypeStruct((full * CANDS, BLOCK), BF16)
    vmem = pl.BlockSpec(memory_space=pltpu.VMEM)
    return pl.pallas_call(
        rows_kernel,
        out_shape=[one] * NY,
        in_specs=[pl.BlockSpec(memory_space=pltpu.SMEM)] + [vmem] * 5,
        out_specs=[vmem] * NY,
        compiler_params=pltpu.CompilerParams(vmem_limit_bytes=8 << 20),
        cost_estimate=pl.CostEstimate(flops=2 * 10**9, transcendentals=0, bytes_accessed=4 << 20),
        name="score_rows",
    )(place, *gathered, impact)


def score_kernel(pos_ref, impact_ref, dense_ref, *refs, extra, steps):
    piece_refs = refs[:6]
    extra_refs = refs[6:10] if extra else ()
    out_refs = refs[-NZ - 3 : -3]
    made_ref, own_ref, own_sem = refs[-3:]
    x, z, core = pos_ref[0], pos_ref[1], pos_ref[2]
    depth, share = piece_refs[0].shape
    chunk = made_ref.shape[1]
    rows = chunk // steps
    half = LANES // 2
    copies = []
    for i in range(2):
        at = (pl.ds((core ^ i) * depth, depth), pl.ds(x * share, share))
        copies.append(pltpu.make_async_copy(impact_ref.at[at], own_ref.at[i], own_sem.at[i]))
        copies[i].start()
    left = lax.broadcasted_iota(jnp.int32, (rows, LANES), 1) < half
    for step in range(steps):
        made = [None, None]
        for i in (2, 3, 4, 5, 6, 7, 0, 1):
            if step == 0 and i == 0:
                for copy in copies:
                    copy.wait()
            piece = own_ref[i] if i < 2 else piece_refs[i - 2][...]
            for part in range(2):
                first = part * chunk + step * rows
                block = dense_ref[first : first + rows, i * depth : (i + 1) * depth]
                one = jnp.dot(block, piece, preferred_element_type=F32)
                made[part] = one if made[part] is None else made[part] + one
        for m in range(NZ // 2):
            a = made[0][:, m * LANES : (m + 1) * LANES]
            b = made[1][:, m * LANES : (m + 1) * LANES]
            at = slice(step * rows, (step + 1) * rows)
            made_ref[2 * m, at, :] = jnp.where(left, a, pltpu.roll(b, half, 1)).astype(BF16)
            made_ref[2 * m + 1, at, :] = jnp.where(left, pltpu.roll(a, half, 1), b).astype(BF16)
    for j, out_ref in enumerate(out_refs):
        out_ref[:chunk, :] = made_ref[(z + j) & (NZ - 1)]
    if extra:
        pack_rows(z, chunk, extra_refs, out_refs)


def pack_rows(z, chunk, extra_refs, out_refs):
    total = extra_refs[0][...].astype(F32)
    for r in extra_refs[1:]:
        total = total + r[...].astype(F32)
    wide, own = LANES // NX, LANES // (NX * NZ)
    deep = total.shape[0] // NZ
    place = (lax.broadcasted_iota(jnp.int32, (deep, LANES), 1) & (wide - 1)) // own
    for j, out_ref in enumerate(out_refs):
        to_z = (z + j) & (NZ - 1)
        packed = jnp.zeros((deep, LANES), F32)
        for g in range(NZ):
            part = total[g * deep : (g + 1) * deep]
            part = pltpu.roll(part, ((g - to_z) * own) & (LANES - 1), 1)
            packed = jnp.where(place == g, part, packed)
        out_ref[chunk:, :] = jnp.concatenate([packed, jnp.zeros_like(packed)], axis=0).astype(BF16)


def score_chunk(place, impact, dense, pieces, sums):
    chunk = dense.shape[0] // 2
    width = dense.shape[1]
    depth, share = pieces[0].shape
    extra = sums is not None
    out_rows = chunk + (2 * sums[0].shape[0] // NZ if extra else 0)
    more = tuple(sums) if extra else ()
    vmem = pl.BlockSpec(memory_space=pltpu.VMEM)
    hbm = pl.BlockSpec(memory_space=pltpu.HBM)
    return pl.pallas_call(
        functools.partial(score_kernel, extra=extra, steps=2),
        out_shape=[jax.ShapeDtypeStruct((out_rows, LANES), BF16)] * NZ,
        in_specs=[pl.BlockSpec(memory_space=pltpu.SMEM), hbm] + [vmem] * (1 + len(pieces) + len(more)),
        out_specs=[vmem] * NZ,
        scratch_shapes=[
            pltpu.VMEM((NZ, chunk, LANES), BF16),
            pltpu.VMEM((2, depth, share), BF16),
            pltpu.SemaphoreType.DMA((2,)),
        ],
        compiler_params=pltpu.CompilerParams(vmem_limit_bytes=12 << 20),
        cost_estimate=pl.CostEstimate(
            flops=2 * chunk * width * share * 2, transcendentals=0, bytes_accessed=chunk * width * 4
        ),
        name="score_chunk",
    )(place, kept_in_hbm(impact), dense, *pieces, *more)


def cut_kernel(pos_ref, impact_ref, query_ref, named_ref, *refs, shifts):
    rows_ref, out_refs, named_here, sem = refs[0], refs[1:-2], refs[-2], refs[-1]
    x, core = pos_ref[0], pos_ref[2]
    full, width = query_ref.shape
    count = len(out_refs) * CUTS
    copies = [
        pltpu.make_async_copy(named_ref, named_here, sem.at[count]),
        pltpu.make_async_copy(query_ref, rows_ref.at[:, pl.ds(0, width)], sem.at[count + 1]),
    ]
    for i, (out_ref, r) in enumerate(zip(out_refs, shifts)):
        depth, share = out_ref.shape
        part = depth // CUTS
        to_x = (x - r) & (NX - 1)
        for j in range(CUTS):
            at = (pl.ds(core * depth + j * part, part), pl.ds(to_x * share, share))
            copies.append(
                pltpu.make_async_copy(impact_ref.at[at], out_ref.at[pl.ds(j * part, part)], sem.at[i * CUTS + j])
            )
    for copy in copies:
        copy.start()
    copies[0].wait()
    named = named_here[...].astype(F32)
    named = jnp.concatenate([named, jnp.zeros((LANES - CANDS, full), F32)], axis=0)
    rows_ref[:, width:] = named.T.astype(BF16)
    for copy in copies[1:]:
        copy.wait()


def cut_slices(place, impact, query_rows, candidates, shifts):
    full, width = query_rows.shape
    one = jax.ShapeDtypeStruct((impact.shape[0] // 2, impact.shape[1] // NX), BF16)
    vmem = pl.BlockSpec(memory_space=pltpu.VMEM)
    hbm = pl.BlockSpec(memory_space=pltpu.HBM)
    rows, *cuts = pl.pallas_call(
        functools.partial(cut_kernel, shifts=shifts),
        out_shape=[jax.ShapeDtypeStruct((full, width + LANES), BF16)] + [one] * len(shifts),
        in_specs=[pl.BlockSpec(memory_space=pltpu.SMEM), hbm, hbm, hbm],
        out_specs=[vmem] * (1 + len(shifts)),
        scratch_shapes=[
            pltpu.VMEM((CANDS, full), jnp.int32),
            pltpu.SemaphoreType.DMA((len(shifts) * CUTS + 2,)),
        ],
        compiler_params=pltpu.CompilerParams(vmem_limit_bytes=4 << 20),
        name="cut_slices",
    )(place, kept_in_hbm(impact), kept_in_hbm(query_rows), kept_in_hbm(candidates.T))
    return rows, cuts


def final_kernel(pos_ref, a0, a1, a2, b0, b1, b2, v0, v1, v2, v3, first_ref, rescored_ref):
    x = pos_ref[0]
    half = LANES // 2
    chunk = b0.shape[0]
    column = 0
    for own, one, two in ((a0, a1, a2), (b0, b1, b2)):
        total = own[:chunk].astype(F32) + one[:chunk].astype(F32) + two[:chunk].astype(F32)
        turned = total.T.astype(BF16)
        first_ref[:, column : column + chunk] = turned[:half]
        first_ref[:, column + chunk : column + 2 * chunk] = turned[half:]
        column += 2 * chunk
    more = v0[...].astype(F32) + v1[...].astype(F32) + v2[...].astype(F32) + v3[...].astype(F32)
    share = LANES // (NX * NZ)
    deep = more.shape[0] // 2
    turned = pltpu.roll(more, (LANES - x * (LANES // NX)) & (LANES - 1), 1).T
    for g in range(NZ):
        part = turned[g * share : (g + 1) * share, :deep]
        rescored_ref[g // 2, :, (g % 2) * deep : (g % 2 + 1) * deep] = part


def finish(place, parts, sums, full):
    chunk = parts[3].shape[0]
    vmem = pl.BlockSpec(memory_space=pltpu.VMEM)
    return pl.pallas_call(
        final_kernel,
        out_shape=[
            jax.ShapeDtypeStruct((LANES // 2, 4 * chunk), BF16),
            jax.ShapeDtypeStruct((CANDS, LANES // (NX * NZ), full), F32),
        ],
        in_specs=[pl.BlockSpec(memory_space=pltpu.SMEM)] + [vmem] * 10,
        out_specs=[vmem] * 2,
        compiler_params=pltpu.CompilerParams(vmem_limit_bytes=8 << 20),
        name="finish",
    )(place, *parts, *sums)


def added(*parts):
    total = parts[0].astype(F32)
    for part in parts[1:]:
        total = total + part.astype(F32)
    return total.astype(BF16)


def after(values, done):
    return lax.optimization_barrier((values, done))[0]


def sent(values):
    out = {}
    for way in (1, -1):
        out[way] = shifted(values[way], "z", way)
    return out


def first_step(made, long_way):
    ahead = shifted(made[4], "z", 2 * long_way)
    return ahead, sent({1: made[3], -1: made[5]})


def second_values(made, long_way, ahead, carried):
    values = {1: [carried[1], made[2]], -1: [carried[-1], made[6]]}
    values[long_way].append(ahead)
    return {way: added(*parts) for way, parts in values.items()}


def third_values(made, carried):
    return {1: added(carried[1], made[1]), -1: added(carried[-1], made[7])}


def rings(made_a, made_b, start_a, start_b):
    (ahead_a, going_a), (ahead_b, going_b) = start_a, start_b
    going_a = sent(second_values(made_a, 1, ahead_a, going_a))
    going_b = sent(second_values(made_b, -1, ahead_b, going_b))
    going_a = sent(third_values(made_a, going_a))
    going_b = sent(third_values(made_b, going_b))
    return (going_a[1], going_a[-1]), (going_b[1], going_b[-1])


def scored(term_ids, term_weights, impact, query_rows, candidates):
    x = lax.axis_index("x")
    z = lax.axis_index("z")
    y = lax.axis_index("prange")
    core = lax.axis_index("query")
    place = jnp.stack([x, z, core, y]).astype(jnp.int32)
    shard_width = impact.shape[0]
    full = query_rows.shape[0]

    shifts = (1, 3, 2)
    rows, cuts = cut_slices(place, impact, query_rows, candidates, shifts)
    near = {r: shifted(one, "x", -r) for r, one in zip(shifts, cuts)}
    (term_ids, term_weights), rows = lax.optimization_barrier(((term_ids, term_weights), rows))
    gathered = [rows] + [shifted(rows, "prange", -r) for r in (1, 2, 3)]

    ids = term_ids.T
    weights = term_weights.T
    half = ids.shape[1] // CHUNKS
    dense_a = build_dense(place, ids[:, :half], weights[:, :half], NX * shard_width)
    gathered = after(gathered, dense_a)
    by_home = score_rows(place, gathered, impact)
    back = [by_home[0]] + [shifted(by_home[r], "prange", r) for r in (1, 2, 3)]
    ids = after(ids, by_home)
    dense_b = build_dense(place, ids[:, half:], weights[:, half:], NX * shard_width)

    near, back = after((near, back), dense_b)
    pieces = []
    for r in (1, 2, 3):
        pieces += [near[r], shifted(near[r], "query", 1)]
    made_a = score_chunk(place, impact, dense_a, pieces, back)
    start_a = first_step(made_a, 1)
    made_b = score_chunk(place, impact, dense_b, pieces, None)
    start_b = first_step(made_b, -1)
    (a1, a2), (b1, b2) = rings(made_a, made_b, start_a, start_b)
    chunk = made_b[0].shape[0]
    mine = added(made_a[0][chunk:], a1[chunk:], a2[chunk:])
    sums = [mine]
    for r in (1, 2, 3):
        sums.append(shifted(mine, "x", r))
    first, rescored = finish(place, (made_a[0], a1, a2, made_b[0], b1, b2), sums, full)
    return (first[None], jnp.transpose(rescored, (2, 0, 1)))


def solution(mesh):
    finer = Mesh(
        mesh.devices.reshape(NX, NZ, mesh.shape["prange"], mesh.shape["query"]),
        ("x", "z", "prange", "query"),
    )
    vocab = ("x", "z")
    in_specs = (
        P("query", None),
        P("query", None),
        P(vocab, "prange"),
        P(("prange", "query"), vocab),
        P(("prange", "query"), None),
    )
    out_specs = (P("prange", vocab, "query"), P(("prange", "query"), None, vocab))
    return jax.shard_map(scored, mesh=finer, in_specs=in_specs, out_specs=out_specs, check_vma=False)
```

```python
import functools

import jax
import jax.numpy as jnp
from jax import lax
from jax.experimental import pallas as pl
from jax.experimental.pallas import tpu as pltpu
from jax.sharding import Mesh
from jax.sharding import PartitionSpec as P


BLOCK = 128
CANDS = 4
NX = 4
NZ = 8
NY = 4
LANES = 128
GROUP = 8
FIRST = 256
CHUNKS = 2
UNROLL = 32
CUTS = 16
F32 = jnp.float32
BF16 = jnp.bfloat16


def shifted(array, axis, shift):
    size = lax.axis_size(axis)
    return lax.ppermute(array, axis, [(i, (i + shift) % size) for i in range(size)])


def kept_in_hbm(array):
    return pltpu.with_memory_space_constraint(array, pltpu.HBM)


def dense_kernel(pos_ref, ids_ref, weights_ref, dense_ref, turned_ref, low_ref, key_ref, weight_ref, *, first):
    x, z, core = pos_ref[0], pos_ref[1], pos_ref[2]
    terms, queries = ids_ref.shape[0], dense_ref.shape[0]
    groups, pairs = low_ref.shape
    highs = dense_ref.shape[1] // FIRST
    ids = ids_ref[:, first : first + queries]
    x_rel = ((ids >> 13) - x) & (NX - 1)
    half_rel = ((ids >> 9) & 1) ^ core
    high = x_rel * 4 + half_rel * 2 + ((ids >> 8) & 1)
    key = high * GROUP + (lax.broadcasted_iota(jnp.int32, ids.shape, 1) & (GROUP - 1))
    key = jnp.where(((ids >> 10) & (NZ - 1)) == z, key, -1)
    low = (ids & (FIRST - 1)).astype(F32)
    weights = weights_ref[:, first : first + queries].astype(F32)
    turned_ref[...] = jnp.concatenate([low, key.astype(F32), weights, weights], axis=0).T
    place = lax.broadcasted_iota(jnp.int32, (groups, LANES), 1) // terms
    across = LANES // terms
    for kind, to_ref in enumerate((low_ref, key_ref, weight_ref)):
        for side in range(pairs // LANES):
            row = None
            for j in range(across):
                part = turned_ref[pl.ds(side * across + j, groups, stride=GROUP), :]
                shift = (terms * (j - kind)) % LANES
                part = pltpu.roll(part, shift, 1) if shift else part
                row = part if row is None else jnp.where(place == j, part, row)
            to_ref[:, side * LANES : (side + 1) * LANES] = row
    low_rows = lax.broadcasted_iota(jnp.int32, (FIRST, pairs), 0).astype(F32).astype(BF16)
    key_rows = lax.broadcasted_iota(jnp.int32, (highs * GROUP, pairs), 0).astype(F32).astype(BF16)
    one = jnp.ones((), BF16)
    zero = jnp.zeros((), BF16)

    def one_group(g):
        low = low_ref[pl.ds(g, 1), :].astype(BF16)
        keys = key_ref[pl.ds(g, 1), :].astype(BF16)
        weights = weight_ref[pl.ds(g, 1), :].astype(BF16)
        ones = jnp.where(low_rows == low, one, zero)
        spread = jnp.where(key_rows == keys, weights, zero)
        made = lax.dot_general(spread, ones, (((1,), (1,)), ((), ())), preferred_element_type=F32)
        return made.reshape(highs, GROUP, FIRST)

    def pair_of_groups(i, carry):
        both = jnp.concatenate([one_group(2 * i), one_group(2 * i + 1)], axis=1).astype(BF16)
        row = pl.multiple_of(i * 2 * GROUP, 2 * GROUP)
        for h in range(highs):
            dense_ref[pl.ds(row, 2 * GROUP), h * FIRST : (h + 1) * FIRST] = both[h]
        return carry

    lax.fori_loop(0, groups // 2, pair_of_groups, 0, unroll=UNROLL)


def build_dense(place, ids, weights, width, chunk):
    terms = ids.shape[0]
    queries = ids.shape[1] // CHUNKS
    groups = queries // GROUP
    rows = pltpu.VMEM((groups, GROUP * terms), F32)
    vmem = pl.BlockSpec(memory_space=pltpu.VMEM)
    return pl.pallas_call(
        functools.partial(dense_kernel, first=chunk * queries),
        out_shape=pltpu.VMEM((queries, width), BF16),
        in_specs=[pl.BlockSpec(memory_space=pltpu.SMEM), vmem, vmem],
        out_specs=vmem,
        scratch_shapes=[pltpu.VMEM((queries, LANES), F32), rows, rows, rows],
        compiler_params=pltpu.CompilerParams(vmem_limit_bytes=6 << 20),
        cost_estimate=pl.CostEstimate(flops=10**10, transcendentals=0, bytes_accessed=queries * width * 2),
        name="dense_build",
    )(place, ids, weights)


def rows_kernel(pos_ref, r0, r1, r2, r3, impact_ref, o0, o1, o2, o3):
    y = pos_ref[3]
    width = impact_ref.shape[0]
    full = r0.shape[0]
    rows = jnp.concatenate([r[:, :width] for r in (r0, r1, r2, r3)], axis=0)
    scores = jnp.dot(rows, impact_ref[...], preferred_element_type=F32)
    blocks = impact_ref.shape[1] // BLOCK
    for home, (r, o) in enumerate(((r0, o0), (r1, o1), (r2, o2), (r3, o3))):
        named = r[:, width : width + LANES].astype(F32).astype(jnp.int32) - y * blocks
        mine = scores[home * full : (home + 1) * full]
        for c in range(CANDS):
            column = named[:, c : c + 1]
            picked = jnp.zeros((full, BLOCK), F32)
            for b in range(blocks):
                picked = jnp.where(column == b, mine[:, b * BLOCK : (b + 1) * BLOCK], picked)
            o[c * full : (c + 1) * full, :] = picked.astype(BF16)


def score_rows(place, gathered, impact):
    full = gathered[0].shape[0]
    one = jax.ShapeDtypeStruct((full * CANDS, BLOCK), BF16)
    vmem = pl.BlockSpec(memory_space=pltpu.VMEM)
    return pl.pallas_call(
        rows_kernel,
        out_shape=[one] * NY,
        in_specs=[pl.BlockSpec(memory_space=pltpu.SMEM)] + [vmem] * 5,
        out_specs=[vmem] * NY,
        compiler_params=pltpu.CompilerParams(vmem_limit_bytes=8 << 20),
        cost_estimate=pl.CostEstimate(flops=2 * 10**9, transcendentals=0, bytes_accessed=4 << 20),
        name="score_rows",
    )(place, *gathered, impact)


def score_kernel(pos_ref, impact_ref, dense_ref, *refs, extra, steps):
    piece_refs = refs[:6]
    extra_refs = refs[6:10] if extra else ()
    own_out, right_out, left_out, ahead_out, pair_right, pair_left = refs[-9:-3]
    made_ref, own_ref, own_sem = refs[-3:]
    x, z, core = pos_ref[0], pos_ref[1], pos_ref[2]
    depth, share = piece_refs[0].shape
    chunk = made_ref.shape[1]
    rows = chunk // steps
    half = LANES // 2
    copies = []
    for i in range(2):
        at = (pl.ds((core ^ i) * depth, depth), pl.ds(x * share, share))
        copies.append(pltpu.make_async_copy(impact_ref.at[at], own_ref.at[i], own_sem.at[i]))
        copies[i].start()
    left = lax.broadcasted_iota(jnp.int32, (rows, LANES), 1) < half
    for step in range(steps):
        made = [None, None]
        for i in (2, 3, 4, 5, 6, 7, 0, 1):
            if step == 0 and i == 0:
                for copy in copies:
                    copy.wait()
            piece = own_ref[i] if i < 2 else piece_refs[i - 2][...]
            for part in range(2):
                first = part * chunk + step * rows
                block = dense_ref[first : first + rows, i * depth : (i + 1) * depth]
                one = jnp.dot(block, piece, preferred_element_type=F32)
                made[part] = one if made[part] is None else made[part] + one
        for m in range(NZ // 2):
            a = made[0][:, m * LANES : (m + 1) * LANES]
            b = made[1][:, m * LANES : (m + 1) * LANES]
            at = slice(step * rows, (step + 1) * rows)
            made_ref[2 * m, at, :] = jnp.where(left, a, pltpu.roll(b, half, 1)).astype(BF16)
            made_ref[2 * m + 1, at, :] = jnp.where(left, pltpu.roll(a, half, 1), b).astype(BF16)
    out_refs = [
        own_out,
        pair_right.at[1],
        right_out,
        pair_right.at[0],
        ahead_out,
        pair_left.at[0],
        left_out,
        pair_left.at[1],
    ]
    for j, out_ref in enumerate(out_refs):
        out_ref[:chunk, :] = made_ref[(z + j) & (NZ - 1)]
    if extra:
        pack_rows(z, chunk, extra_refs, out_refs)


def pack_rows(z, chunk, extra_refs, out_refs):
    total = extra_refs[0][...].astype(F32)
    for r in extra_refs[1:]:
        total = total + r[...].astype(F32)
    wide, own = LANES // NX, LANES // (NX * NZ)
    deep = total.shape[0] // NZ
    place = (lax.broadcasted_iota(jnp.int32, (deep, LANES), 1) & (wide - 1)) // own
    for j, out_ref in enumerate(out_refs):
        to_z = (z + j) & (NZ - 1)
        packed = jnp.zeros((deep, LANES), F32)
        for g in range(NZ):
            part = total[g * deep : (g + 1) * deep]
            part = pltpu.roll(part, ((g - to_z) * own) & (LANES - 1), 1)
            packed = jnp.where(place == g, part, packed)
        out_ref[chunk:, :] = jnp.concatenate([packed, jnp.zeros_like(packed)], axis=0).astype(BF16)


def score_chunk(place, impact, dense, pieces, sums):
    chunk = dense.shape[0] // 2
    width = dense.shape[1]
    depth, share = pieces[0].shape
    extra = sums is not None
    out_rows = chunk + (2 * sums[0].shape[0] // NZ if extra else 0)
    more = tuple(sums) if extra else ()
    vmem = pl.BlockSpec(memory_space=pltpu.VMEM)
    hbm = pl.BlockSpec(memory_space=pltpu.HBM)
    return pl.pallas_call(
        functools.partial(score_kernel, extra=extra, steps=2),
        out_shape=[jax.ShapeDtypeStruct((out_rows, LANES), BF16)] * 4
        + [jax.ShapeDtypeStruct((2, out_rows, LANES), BF16)] * 2,
        in_specs=[pl.BlockSpec(memory_space=pltpu.SMEM), hbm] + [vmem] * (1 + len(pieces) + len(more)),
        out_specs=[vmem] * 6,
        scratch_shapes=[
            pltpu.VMEM((NZ, chunk, LANES), BF16),
            pltpu.VMEM((2, depth, share), BF16),
            pltpu.SemaphoreType.DMA((2,)),
        ],
        compiler_params=pltpu.CompilerParams(vmem_limit_bytes=12 << 20),
        cost_estimate=pl.CostEstimate(
            flops=2 * chunk * width * share * 2, transcendentals=0, bytes_accessed=chunk * width * 4
        ),
        name="score_chunk",
    )(place, kept_in_hbm(impact), dense, *pieces, *more)


def cut_kernel(pos_ref, impact_ref, query_ref, named_ref, ids_ref, weights_ref, *refs, shifts):
    rows_ref, ids_here, weights_here = refs[:3]
    out_refs, named_here, sem = refs[3:-2], refs[-2], refs[-1]
    x, core = pos_ref[0], pos_ref[2]
    full, width = query_ref.shape
    count = len(out_refs) * CUTS
    copies = [
        pltpu.make_async_copy(named_ref, named_here, sem.at[count]),
        pltpu.make_async_copy(query_ref, rows_ref.at[:, pl.ds(0, width)], sem.at[count + 1]),
        pltpu.make_async_copy(ids_ref, ids_here, sem.at[count + 2]),
        pltpu.make_async_copy(weights_ref, weights_here, sem.at[count + 3]),
    ]
    for i, (out_ref, r) in enumerate(zip(out_refs, shifts)):
        depth, share = out_ref.shape
        part = depth // CUTS
        to_x = (x - r) & (NX - 1)
        for j in range(CUTS):
            at = (pl.ds(core * depth + j * part, part), pl.ds(to_x * share, share))
            copies.append(
                pltpu.make_async_copy(impact_ref.at[at], out_ref.at[pl.ds(j * part, part)], sem.at[i * CUTS + j])
            )
    for copy in copies:
        copy.start()
    copies[0].wait()
    named = named_here[...].astype(F32)
    named = jnp.concatenate([named, jnp.zeros((LANES - CANDS, full), F32)], axis=0)
    rows_ref[:, width:] = named.T.astype(BF16)
    for copy in copies[1:]:
        copy.wait()


def cut_slices(place, impact, query_rows, candidates, ids, weights, shifts):
    full, width = query_rows.shape
    one = jax.ShapeDtypeStruct((impact.shape[0] // 2, impact.shape[1] // NX), BF16)
    vmem = pl.BlockSpec(memory_space=pltpu.VMEM)
    hbm = pl.BlockSpec(memory_space=pltpu.HBM)
    rows, ids_here, weights_here, *cuts = pl.pallas_call(
        functools.partial(cut_kernel, shifts=shifts),
        out_shape=[
            jax.ShapeDtypeStruct((full, width + LANES), BF16),
            jax.ShapeDtypeStruct(ids.shape, ids.dtype),
            jax.ShapeDtypeStruct(weights.shape, weights.dtype),
        ]
        + [one] * len(shifts),
        in_specs=[pl.BlockSpec(memory_space=pltpu.SMEM)] + [hbm] * 5,
        out_specs=[vmem] * (3 + len(shifts)),
        scratch_shapes=[
            pltpu.VMEM((CANDS, full), jnp.int32),
            pltpu.SemaphoreType.DMA((len(shifts) * CUTS + 4,)),
        ],
        compiler_params=pltpu.CompilerParams(vmem_limit_bytes=4 << 20),
        name="cut_slices",
    )(place, *[kept_in_hbm(a) for a in (impact, query_rows, candidates.T, ids, weights)])
    return rows, ids_here, weights_here, cuts


def final_kernel(pos_ref, *refs):
    v0, v1, v2, v3, first_ref, rescored_ref = refs[10:]
    x = pos_ref[0]
    half = LANES // 2
    chunk = first_ref.shape[1] // 4
    column = 0
    for own, right, left, far_right, far_left in (refs[:5], refs[5:10]):
        total = own[:chunk].astype(F32) + right[1, :chunk].astype(F32) + left[1, :chunk].astype(F32)
        total = total + far_right[:chunk].astype(F32) + far_left[:chunk].astype(F32)
        turned = total.T.astype(BF16)
        first_ref[:, column : column + chunk] = turned[:half]
        first_ref[:, column + chunk : column + 2 * chunk] = turned[half:]
        column += 2 * chunk
    more = v0[...].astype(F32) + v1[...].astype(F32) + v2[...].astype(F32) + v3[...].astype(F32)
    share = LANES // (NX * NZ)
    deep = more.shape[0] // 2
    turned = pltpu.roll(more, (LANES - x * (LANES // NX)) & (LANES - 1), 1).T
    for g in range(NZ):
        part = turned[g * share : (g + 1) * share, :deep]
        rescored_ref[g // 2, :, (g % 2) * deep : (g % 2 + 1) * deep] = part


def finish(place, parts, sums, full):
    chunk = parts[5].shape[0]
    vmem = pl.BlockSpec(memory_space=pltpu.VMEM)
    return pl.pallas_call(
        final_kernel,
        out_shape=[
            jax.ShapeDtypeStruct((LANES // 2, 4 * chunk), BF16),
            jax.ShapeDtypeStruct((CANDS, LANES // (NX * NZ), full), F32),
        ],
        in_specs=[pl.BlockSpec(memory_space=pltpu.SMEM)] + [vmem] * 14,
        out_specs=[vmem] * 2,
        compiler_params=pltpu.CompilerParams(vmem_limit_bytes=8 << 20),
        name="finish",
    )(place, *parts, *sums)


def added(*parts):
    total = parts[0].astype(F32)
    for part in parts[1:]:
        total = total + part.astype(F32)
    return total.astype(BF16)


def after(values, done):
    return lax.optimization_barrier((values, done))[0]


def passed(value, way):
    return shifted(value, "z", way)


def first_step(made, long_way):
    ahead = passed(made[3], 2 * long_way)
    return ahead, passed(made[4], 1), passed(made[5], -1)


def second_step(made, long_way, going):
    ahead, right, left = going
    values = {1: [right[0], made[1]], -1: [left[0], made[2]]}
    values[long_way].append(ahead)
    far_right = passed(added(*values[1]), 2)
    far_left = passed(added(*values[-1]), -2)
    return made[0], right, left, far_right, far_left


def scored(term_ids, term_weights, impact, query_rows, candidates):
    x = lax.axis_index("x")
    z = lax.axis_index("z")
    y = lax.axis_index("prange")
    core = lax.axis_index("query")
    place = jnp.stack([x, z, core, y]).astype(jnp.int32)
    shard_width = impact.shape[0]
    full = query_rows.shape[0]

    shifts = (1, 3, 2)
    rows, ids, weights, cuts = cut_slices(place, impact, query_rows, candidates, term_ids.T, term_weights.T, shifts)
    near = {}
    for r, one in zip(shifts, cuts):
        near[r] = shifted(one, "x", -r)
    gathered = [rows]
    for r in (1, 2, 3):
        gathered.append(shifted(rows, "prange", -r))
    dense_a = build_dense(place, ids, weights, NX * shard_width, 0)
    gathered = after(gathered, dense_a)
    by_home = score_rows(place, gathered, impact)
    back = [by_home[0]] + [shifted(by_home[r], "prange", r) for r in (1, 2, 3)]
    ids = after(ids, by_home)
    dense_b = build_dense(place, ids, weights, NX * shard_width, 1)

    near, back = after((near, back), dense_b)
    pieces = []
    for r in (1, 2, 3):
        pieces += [near[r], shifted(near[r], "query", 1)]
    made_a = score_chunk(place, impact, dense_a, pieces, back)
    start_a = first_step(made_a, 1)
    made_b = score_chunk(place, impact, dense_b, pieces, None)
    start_b = first_step(made_b, -1)
    parts_a = second_step(made_a, 1, start_a)
    parts_b = second_step(made_b, -1, start_b)
    chunk = made_b[0].shape[0]
    mine = [part[1] if part.ndim == 3 else part for part in parts_a]
    mine = added(*[part[chunk:] for part in mine])
    sums = [mine]
    for r in (1, 2, 3):
        sums.append(shifted(mine, "x", r))
    first, rescored = finish(place, parts_a + parts_b, sums, full)
    return (first[None], jnp.transpose(rescored, (2, 0, 1)))


def solution(mesh):
    finer = Mesh(
        mesh.devices.reshape(NX, NZ, mesh.shape["prange"], mesh.shape["query"]),
        ("x", "z", "prange", "query"),
    )
    vocab = ("x", "z")
    in_specs = (
        P("query", None),
        P("query", None),
        P(vocab, "prange"),
        P(("prange", "query"), vocab),
        P(("prange", "query"), None),
    )
    out_specs = (P("prange", vocab, "query"), P(("prange", "query"), None, vocab))
    return jax.shard_map(scored, mesh=finer, in_specs=in_specs, out_specs=out_specs, check_vma=False)
```

```python
import functools

import jax
import jax.numpy as jnp
from jax import lax
from jax.experimental import pallas as pl
from jax.experimental.pallas import tpu as pltpu
from jax.sharding import Mesh
from jax.sharding import PartitionSpec as P


BLOCK = 128
CANDS = 4
NX = 4
NZ = 8
NY = 4
LANES = 128
GROUP = 8
FIRST = 256
CHUNKS = 2
UNROLL = 32
CUTS = 16
F32 = jnp.float32
BF16 = jnp.bfloat16


def shifted(array, axis, shift):
    size = lax.axis_size(axis)
    return lax.ppermute(array, axis, [(i, (i + shift) % size) for i in range(size)])


def kept_in_hbm(array):
    return pltpu.with_memory_space_constraint(array, pltpu.HBM)


def dense_kernel(pos_ref, ids_ref, weights_ref, dense_ref, turned_ref, low_ref, key_ref, weight_ref, *, first):
    x, z, core = pos_ref[0], pos_ref[1], pos_ref[2]
    terms, queries = ids_ref.shape[0], dense_ref.shape[0]
    groups, pairs = low_ref.shape
    highs = dense_ref.shape[1] // FIRST
    ids = ids_ref[:, first : first + queries]
    x_rel = ((ids >> 13) - x) & (NX - 1)
    half_rel = ((ids >> 9) & 1) ^ core
    high = x_rel * 4 + half_rel * 2 + ((ids >> 8) & 1)
    key = high * GROUP + (lax.broadcasted_iota(jnp.int32, ids.shape, 1) & (GROUP - 1))
    key = jnp.where(((ids >> 10) & (NZ - 1)) == z, key, -1)
    low = (ids & (FIRST - 1)).astype(F32)
    weights = weights_ref[:, first : first + queries].astype(F32)
    turned_ref[...] = jnp.concatenate([low, key.astype(F32), weights, weights], axis=0).T
    place = lax.broadcasted_iota(jnp.int32, (groups, LANES), 1) // terms
    across = LANES // terms
    for kind, to_ref in enumerate((low_ref, key_ref, weight_ref)):
        for side in range(pairs // LANES):
            row = None
            for j in range(across):
                part = turned_ref[pl.ds(side * across + j, groups, stride=GROUP), :]
                shift = (terms * (j - kind)) % LANES
                part = pltpu.roll(part, shift, 1) if shift else part
                row = part if row is None else jnp.where(place == j, part, row)
            to_ref[:, side * LANES : (side + 1) * LANES] = row
    low_rows = lax.broadcasted_iota(jnp.int32, (FIRST, pairs), 0).astype(F32).astype(BF16)
    key_rows = lax.broadcasted_iota(jnp.int32, (highs * GROUP, pairs), 0).astype(F32).astype(BF16)
    one = jnp.ones((), BF16)
    zero = jnp.zeros((), BF16)

    def one_group(g):
        low = low_ref[pl.ds(g, 1), :].astype(BF16)
        keys = key_ref[pl.ds(g, 1), :].astype(BF16)
        weights = weight_ref[pl.ds(g, 1), :].astype(BF16)
        ones = jnp.where(low_rows == low, one, zero)
        spread = jnp.where(key_rows == keys, weights, zero)
        made = lax.dot_general(spread, ones, (((1,), (1,)), ((), ())), preferred_element_type=F32)
        return made.reshape(highs, GROUP, FIRST)

    def pair_of_groups(i, carry):
        both = jnp.concatenate([one_group(2 * i), one_group(2 * i + 1)], axis=1).astype(BF16)
        row = pl.multiple_of(i * 2 * GROUP, 2 * GROUP)
        for h in range(highs):
            dense_ref[pl.ds(row, 2 * GROUP), h * FIRST : (h + 1) * FIRST] = both[h]
        return carry

    lax.fori_loop(0, groups // 2, pair_of_groups, 0, unroll=UNROLL)


def build_dense(place, ids, weights, width, chunk):
    terms = ids.shape[0]
    queries = ids.shape[1] // CHUNKS
    groups = queries // GROUP
    rows = pltpu.VMEM((groups, GROUP * terms), F32)
    vmem = pl.BlockSpec(memory_space=pltpu.VMEM)
    return pl.pallas_call(
        functools.partial(dense_kernel, first=chunk * queries),
        out_shape=pltpu.VMEM((queries, width), BF16),
        in_specs=[pl.BlockSpec(memory_space=pltpu.SMEM), vmem, vmem],
        out_specs=vmem,
        scratch_shapes=[pltpu.VMEM((queries, LANES), F32), rows, rows, rows],
        compiler_params=pltpu.CompilerParams(vmem_limit_bytes=6 << 20),
        cost_estimate=pl.CostEstimate(flops=10**10, transcendentals=0, bytes_accessed=queries * width * 2),
        name="dense_build",
    )(place, ids, weights)


def rows_kernel(pos_ref, r0, r1, r2, r3, impact_ref, o0, o1, o2, o3):
    y = pos_ref[3]
    width = impact_ref.shape[0]
    full = r0.shape[0]
    rows = jnp.concatenate([r[:, :width] for r in (r0, r1, r2, r3)], axis=0)
    scores = jnp.dot(rows, impact_ref[...], preferred_element_type=F32)
    blocks = impact_ref.shape[1] // BLOCK
    for home, (r, o) in enumerate(((r0, o0), (r1, o1), (r2, o2), (r3, o3))):
        named = r[:, width : width + LANES].astype(F32).astype(jnp.int32) - y * blocks
        mine = scores[home * full : (home + 1) * full]
        for c in range(CANDS):
            column = named[:, c : c + 1]
            picked = jnp.zeros((full, BLOCK), F32)
            for b in range(blocks):
                picked = jnp.where(column == b, mine[:, b * BLOCK : (b + 1) * BLOCK], picked)
            o[c * full : (c + 1) * full, :] = picked.astype(BF16)


def score_rows(place, gathered, impact):
    full = gathered[0].shape[0]
    one = jax.ShapeDtypeStruct((full * CANDS, BLOCK), BF16)
    vmem = pl.BlockSpec(memory_space=pltpu.VMEM)
    return pl.pallas_call(
        rows_kernel,
        out_shape=[one] * NY,
        in_specs=[pl.BlockSpec(memory_space=pltpu.SMEM)] + [vmem] * 5,
        out_specs=[vmem] * NY,
        compiler_params=pltpu.CompilerParams(vmem_limit_bytes=8 << 20),
        cost_estimate=pl.CostEstimate(flops=2 * 10**9, transcendentals=0, bytes_accessed=4 << 20),
        name="score_rows",
    )(place, *gathered, impact)


def score_kernel(pos_ref, impact_ref, dense_ref, *refs, extra, steps):
    piece_refs = refs[:6]
    extra_refs = refs[6:10] if extra else ()
    out_refs = refs[-NZ - 3 : -3]
    made_ref, own_ref, own_sem = refs[-3:]
    x, z, core = pos_ref[0], pos_ref[1], pos_ref[2]
    depth, share = piece_refs[0].shape
    chunk = made_ref.shape[1]
    rows = chunk // steps
    half = LANES // 2
    copies = []
    for i in range(2):
        at = (pl.ds((core ^ i) * depth, depth), pl.ds(x * share, share))
        copies.append(pltpu.make_async_copy(impact_ref.at[at], own_ref.at[i], own_sem.at[i]))
        copies[i].start()
    left = lax.broadcasted_iota(jnp.int32, (rows, LANES), 1) < half
    for step in range(steps):
        made = [None, None]
        for i in (2, 3, 4, 5, 6, 7, 0, 1):
            if step == 0 and i == 0:
                for copy in copies:
                    copy.wait()
            piece = own_ref[i] if i < 2 else piece_refs[i - 2][...]
            for part in range(2):
                first = part * chunk + step * rows
                block = dense_ref[first : first + rows, i * depth : (i + 1) * depth]
                one = jnp.dot(block, piece, preferred_element_type=F32)
                made[part] = one if made[part] is None else made[part] + one
        for m in range(NZ // 2):
            a = made[0][:, m * LANES : (m + 1) * LANES]
            b = made[1][:, m * LANES : (m + 1) * LANES]
            at = slice(step * rows, (step + 1) * rows)
            made_ref[2 * m, at, :] = jnp.where(left, a, pltpu.roll(b, half, 1)).astype(BF16)
            made_ref[2 * m + 1, at, :] = jnp.where(left, pltpu.roll(a, half, 1), b).astype(BF16)
    for j, out_ref in enumerate(out_refs):
        out_ref[:chunk, :] = made_ref[(z + j) & (NZ - 1)]
    if extra:
        pack_rows(z, chunk, extra_refs, out_refs)


def pack_rows(z, chunk, extra_refs, out_refs):
    total = extra_refs[0][...].astype(F32)
    for r in extra_refs[1:]:
        total = total + r[...].astype(F32)
    wide, own = LANES // NX, LANES // (NX * NZ)
    deep = total.shape[0] // NZ
    place = (lax.broadcasted_iota(jnp.int32, (deep, LANES), 1) & (wide - 1)) // own
    for j, out_ref in enumerate(out_refs):
        to_z = (z + j) & (NZ - 1)
        packed = jnp.zeros((deep, LANES), F32)
        for g in range(NZ):
            part = total[g * deep : (g + 1) * deep]
            part = pltpu.roll(part, ((g - to_z) * own) & (LANES - 1), 1)
            packed = jnp.where(place == g, part, packed)
        out_ref[chunk:, :] = jnp.concatenate([packed, jnp.zeros_like(packed)], axis=0).astype(BF16)


def score_chunk(place, impact, dense, pieces, sums):
    chunk = dense.shape[0] // 2
    width = dense.shape[1]
    depth, share = pieces[0].shape
    extra = sums is not None
    out_rows = chunk + (2 * sums[0].shape[0] // NZ if extra else 0)
    more = tuple(sums) if extra else ()
    vmem = pl.BlockSpec(memory_space=pltpu.VMEM)
    hbm = pl.BlockSpec(memory_space=pltpu.HBM)
    return pl.pallas_call(
        functools.partial(score_kernel, extra=extra, steps=2),
        out_shape=[jax.ShapeDtypeStruct((out_rows, LANES), BF16)] * NZ,
        in_specs=[pl.BlockSpec(memory_space=pltpu.SMEM), hbm] + [vmem] * (1 + len(pieces) + len(more)),
        out_specs=[vmem] * NZ,
        scratch_shapes=[
            pltpu.VMEM((NZ, chunk, LANES), BF16),
            pltpu.VMEM((2, depth, share), BF16),
            pltpu.SemaphoreType.DMA((2,)),
        ],
        compiler_params=pltpu.CompilerParams(vmem_limit_bytes=12 << 20),
        cost_estimate=pl.CostEstimate(
            flops=2 * chunk * width * share * 2, transcendentals=0, bytes_accessed=chunk * width * 4
        ),
        name="score_chunk",
    )(place, kept_in_hbm(impact), dense, *pieces, *more)


def cut_kernel(pos_ref, impact_ref, query_ref, named_ref, ids_ref, weights_ref, *refs, shifts):
    rows_ref, ids_here, weights_here = refs[:3]
    out_refs, named_here, sem = refs[3:-2], refs[-2], refs[-1]
    x, core = pos_ref[0], pos_ref[2]
    full, width = query_ref.shape
    count = len(out_refs) * CUTS
    copies = [
        pltpu.make_async_copy(named_ref, named_here, sem.at[count]),
        pltpu.make_async_copy(query_ref, rows_ref.at[:, pl.ds(0, width)], sem.at[count + 1]),
        pltpu.make_async_copy(ids_ref, ids_here, sem.at[count + 2]),
        pltpu.make_async_copy(weights_ref, weights_here, sem.at[count + 3]),
    ]
    for i, (out_ref, r) in enumerate(zip(out_refs, shifts)):
        depth, share = out_ref.shape
        part = depth // CUTS
        to_x = (x - r) & (NX - 1)
        for j in range(CUTS):
            at = (pl.ds(core * depth + j * part, part), pl.ds(to_x * share, share))
            copies.append(
                pltpu.make_async_copy(impact_ref.at[at], out_ref.at[pl.ds(j * part, part)], sem.at[i * CUTS + j])
            )
    for copy in copies:
        copy.start()
    copies[0].wait()
    named = named_here[...].astype(F32)
    named = jnp.concatenate([named, jnp.zeros((LANES - CANDS, full), F32)], axis=0)
    rows_ref[:, width:] = named.T.astype(BF16)
    for copy in copies[1:]:
        copy.wait()


def cut_slices(place, impact, query_rows, candidates, ids, weights, shifts):
    full, width = query_rows.shape
    one = jax.ShapeDtypeStruct((impact.shape[0] // 2, impact.shape[1] // NX), BF16)
    vmem = pl.BlockSpec(memory_space=pltpu.VMEM)
    hbm = pl.BlockSpec(memory_space=pltpu.HBM)
    rows, ids_here, weights_here, *cuts = pl.pallas_call(
        functools.partial(cut_kernel, shifts=shifts),
        out_shape=[
            jax.ShapeDtypeStruct((full, width + LANES), BF16),
            jax.ShapeDtypeStruct(ids.shape, ids.dtype),
            jax.ShapeDtypeStruct(weights.shape, weights.dtype),
        ]
        + [one] * len(shifts),
        in_specs=[pl.BlockSpec(memory_space=pltpu.SMEM)] + [hbm] * 5,
        out_specs=[vmem] * (3 + len(shifts)),
        scratch_shapes=[
            pltpu.VMEM((CANDS, full), jnp.int32),
            pltpu.SemaphoreType.DMA((len(shifts) * CUTS + 4,)),
        ],
        compiler_params=pltpu.CompilerParams(vmem_limit_bytes=4 << 20),
        name="cut_slices",
    )(place, *[kept_in_hbm(a) for a in (impact, query_rows, candidates.T, ids, weights)])
    return rows, ids_here, weights_here, cuts


def summed_chunk(parts, to_ref, column):
    half = LANES // 2
    chunk = to_ref.shape[1] // 2 if column is None else to_ref.shape[1] // 4
    column = column or 0
    total = parts[0][:chunk].astype(F32)
    for part in parts[1:]:
        total = total + part[:chunk].astype(F32)
    turned = total.T.astype(BF16)
    to_ref[:, column : column + chunk] = turned[:half]
    to_ref[:, column + chunk : column + 2 * chunk] = turned[half:]


def half_kernel(a0, a1, a2, done_ref):
    summed_chunk((a0, a1, a2), done_ref, None)


def finish_half(parts, chunk):
    vmem = pl.BlockSpec(memory_space=pltpu.VMEM)
    return pl.pallas_call(
        half_kernel,
        out_shape=jax.ShapeDtypeStruct((LANES // 2, 2 * chunk), BF16),
        in_specs=[vmem] * 3,
        out_specs=vmem,
        compiler_params=pltpu.CompilerParams(vmem_limit_bytes=4 << 20),
        name="finish_half",
    )(*parts)


def final_kernel(pos_ref, done_ref, b0, b1, b2, v0, v1, v2, v3, first_ref, rescored_ref):
    x = pos_ref[0]
    columns = done_ref.shape[1]
    first_ref[:, :columns] = done_ref[...]
    summed_chunk((b0, b1, b2), first_ref, columns)
    more = v0[...].astype(F32) + v1[...].astype(F32) + v2[...].astype(F32) + v3[...].astype(F32)
    share = LANES // (NX * NZ)
    deep = more.shape[0] // 2
    turned = pltpu.roll(more, (LANES - x * (LANES // NX)) & (LANES - 1), 1).T
    for g in range(NZ):
        part = turned[g * share : (g + 1) * share, :deep]
        rescored_ref[g // 2, :, (g % 2) * deep : (g % 2 + 1) * deep] = part


def finish(place, done, parts, sums, full):
    vmem = pl.BlockSpec(memory_space=pltpu.VMEM)
    return pl.pallas_call(
        final_kernel,
        out_shape=[
            jax.ShapeDtypeStruct((LANES // 2, 2 * done.shape[1]), BF16),
            jax.ShapeDtypeStruct((CANDS, LANES // (NX * NZ), full), F32),
        ],
        in_specs=[pl.BlockSpec(memory_space=pltpu.SMEM)] + [vmem] * 8,
        out_specs=[vmem] * 2,
        compiler_params=pltpu.CompilerParams(vmem_limit_bytes=8 << 20),
        name="finish",
    )(place, done, *parts, *sums)


def added(*parts):
    total = parts[0].astype(F32)
    for part in parts[1:]:
        total = total + part.astype(F32)
    return total.astype(BF16)


def after(values, done):
    return lax.optimization_barrier((values, done))[0]


def sent(values):
    out = {}
    for way in (1, -1):
        out[way] = shifted(values[way], "z", way)
    return out


def first_step(made, long_way):
    ahead = shifted(made[4], "z", 2 * long_way)
    return ahead, sent({1: made[3], -1: made[5]})


def second_values(made, long_way, ahead, carried):
    values = {1: [carried[1], made[2]], -1: [carried[-1], made[6]]}
    values[long_way].append(ahead)
    return {way: added(*parts) for way, parts in values.items()}


def third_values(made, carried):
    return {1: added(carried[1], made[1]), -1: added(carried[-1], made[7])}


def rings(made_a, made_b, start_a, start_b):
    (ahead_a, going_a), (ahead_b, going_b) = start_a, start_b
    going_a = sent(second_values(made_a, 1, ahead_a, going_a))
    going_b = sent(second_values(made_b, -1, ahead_b, going_b))
    going_a = sent(third_values(made_a, going_a))
    going_b = sent(third_values(made_b, going_b))
    return (going_a[1], going_a[-1]), (going_b[1], going_b[-1])


def scored(term_ids, term_weights, impact, query_rows, candidates):
    x = lax.axis_index("x")
    z = lax.axis_index("z")
    y = lax.axis_index("prange")
    core = lax.axis_index("query")
    place = jnp.stack([x, z, core, y]).astype(jnp.int32)
    shard_width = impact.shape[0]
    full = query_rows.shape[0]

    shifts = (1, 3, 2)
    rows, ids, weights, cuts = cut_slices(place, impact, query_rows, candidates, term_ids.T, term_weights.T, shifts)
    near = {}
    for r, one in zip(shifts, cuts):
        near[r] = shifted(one, "x", -r)
    gathered = [rows]
    for r in (1, 2, 3):
        gathered.append(shifted(rows, "prange", -r))
    dense_a = build_dense(place, ids, weights, NX * shard_width, 0)
    gathered = after(gathered, dense_a)
    by_home = score_rows(place, gathered, impact)
    back = [by_home[0]]
    for r in (1, 2, 3):
        back.append(shifted(by_home[r], "prange", r))
    ids = after(ids, by_home)
    dense_b = build_dense(place, ids, weights, NX * shard_width, 1)

    pieces = {}
    for r in (1, 3, 2):
        ready = after(near[r], dense_b)
        pieces[r] = [ready, shifted(ready, "query", 1)]
    back = after(back, dense_b)
    pieces = pieces[1] + pieces[2] + pieces[3]
    made_a = score_chunk(place, impact, dense_a, pieces, back)
    start_a = first_step(made_a, 1)
    made_b = score_chunk(place, impact, dense_b, pieces, None)
    start_b = first_step(made_b, -1)
    (a1, a2), (b1, b2) = rings(made_a, made_b, start_a, start_b)
    chunk = made_b[0].shape[0]
    mine = added(made_a[0][chunk:], a1[chunk:], a2[chunk:])
    sums = [mine]
    for r in (1, 2, 3):
        sums.append(shifted(mine, "x", r))
    done = finish_half((made_a[0], a1, a2), chunk)
    first, rescored = finish(place, done, (made_b[0], b1, b2), sums, full)
    return (first[None], jnp.transpose(rescored, (2, 0, 1)))


def solution(mesh):
    finer = Mesh(
        mesh.devices.reshape(NX, NZ, mesh.shape["prange"], mesh.shape["query"]),
        ("x", "z", "prange", "query"),
    )
    vocab = ("x", "z")
    in_specs = (
        P("query", None),
        P("query", None),
        P(vocab, "prange"),
        P(("prange", "query"), vocab),
        P(("prange", "query"), None),
    )
    out_specs = (P("prange", vocab, "query"), P(("prange", "query"), None, vocab))
    return jax.shard_map(scored, mesh=finer, in_specs=in_specs, out_specs=out_specs, check_vma=False)
```

```python
import functools

import jax
import jax.numpy as jnp
from jax import lax
from jax.experimental import pallas as pl
from jax.experimental.pallas import tpu as pltpu
from jax.sharding import Mesh
from jax.sharding import PartitionSpec as P


BLOCK = 128
CANDS = 4
NX = 4
NZ = 8
NY = 4
LANES = 128
GROUP = 8
FIRST = 256
CHUNKS = 2
UNROLL = 32
CUTS = 16
F32 = jnp.float32
BF16 = jnp.bfloat16


def shifted(array, axis, shift):
    size = lax.axis_size(axis)
    return lax.ppermute(array, axis, [(i, (i + shift) % size) for i in range(size)])


def kept_in_hbm(array):
    return pltpu.with_memory_space_constraint(array, pltpu.HBM)


def dense_kernel(pos_ref, ids_ref, weights_ref, dense_ref, turned_ref, low_ref, key_ref, weight_ref, *, first):
    x, z, core = pos_ref[0], pos_ref[1], pos_ref[2]
    terms, queries = ids_ref.shape[0], dense_ref.shape[0]
    groups, pairs = low_ref.shape
    highs = dense_ref.shape[1] // FIRST
    ids = ids_ref[:, first : first + queries]
    x_rel = ((ids >> 13) - x) & (NX - 1)
    half_rel = ((ids >> 9) & 1) ^ core
    high = x_rel * 4 + half_rel * 2 + ((ids >> 8) & 1)
    key = high * GROUP + (lax.broadcasted_iota(jnp.int32, ids.shape, 1) & (GROUP - 1))
    key = jnp.where(((ids >> 10) & (NZ - 1)) == z, key, -1)
    low = (ids & (FIRST - 1)).astype(F32)
    weights = weights_ref[:, first : first + queries].astype(F32)
    turned_ref[...] = jnp.concatenate([low, key.astype(F32), weights, weights], axis=0).T
    place = lax.broadcasted_iota(jnp.int32, (groups, LANES), 1) // terms
    across = LANES // terms
    for kind, to_ref in enumerate((low_ref, key_ref, weight_ref)):
        for side in range(pairs // LANES):
            row = None
            for j in range(across):
                part = turned_ref[pl.ds(side * across + j, groups, stride=GROUP), :]
                shift = (terms * (j - kind)) % LANES
                part = pltpu.roll(part, shift, 1) if shift else part
                row = part if row is None else jnp.where(place == j, part, row)
            to_ref[:, side * LANES : (side + 1) * LANES] = row
    low_rows = lax.broadcasted_iota(jnp.int32, (FIRST, pairs), 0).astype(F32).astype(BF16)
    key_rows = lax.broadcasted_iota(jnp.int32, (highs * GROUP, pairs), 0).astype(F32).astype(BF16)
    one = jnp.ones((), BF16)
    zero = jnp.zeros((), BF16)

    def one_group(g):
        low = low_ref[pl.ds(g, 1), :].astype(BF16)
        keys = key_ref[pl.ds(g, 1), :].astype(BF16)
        weights = weight_ref[pl.ds(g, 1), :].astype(BF16)
        ones = jnp.where(low_rows == low, one, zero)
        spread = jnp.where(key_rows == keys, weights, zero)
        made = lax.dot_general(spread, ones, (((1,), (1,)), ((), ())), preferred_element_type=F32)
        return made.reshape(highs, GROUP, FIRST)

    def pair_of_groups(i, carry):
        both = jnp.concatenate([one_group(2 * i), one_group(2 * i + 1)], axis=1).astype(BF16)
        row = pl.multiple_of(i * 2 * GROUP, 2 * GROUP)
        for h in range(highs):
            dense_ref[pl.ds(row, 2 * GROUP), h * FIRST : (h + 1) * FIRST] = both[h]
        return carry

    lax.fori_loop(0, groups // 2, pair_of_groups, 0, unroll=UNROLL)


def build_dense(place, ids, weights, width, chunk):
    terms = ids.shape[0]
    queries = ids.shape[1] // CHUNKS
    groups = queries // GROUP
    rows = pltpu.VMEM((groups, GROUP * terms), F32)
    vmem = pl.BlockSpec(memory_space=pltpu.VMEM)
    return pl.pallas_call(
        functools.partial(dense_kernel, first=chunk * queries),
        out_shape=pltpu.VMEM((queries, width), BF16),
        in_specs=[pl.BlockSpec(memory_space=pltpu.SMEM), vmem, vmem],
        out_specs=vmem,
        scratch_shapes=[pltpu.VMEM((queries, LANES), F32), rows, rows, rows],
        compiler_params=pltpu.CompilerParams(vmem_limit_bytes=6 << 20),
        cost_estimate=pl.CostEstimate(flops=10**10, transcendentals=0, bytes_accessed=queries * width * 2),
        name="dense_build",
    )(place, ids, weights)


def rows_kernel(pos_ref, r0, r1, r2, r3, impact_ref, o0, o1, o2, o3):
    y = pos_ref[3]
    width = impact_ref.shape[0]
    full = r0.shape[0]
    rows = jnp.concatenate([r[:, :width] for r in (r0, r1, r2, r3)], axis=0)
    scores = jnp.dot(rows, impact_ref[...], preferred_element_type=F32)
    blocks = impact_ref.shape[1] // BLOCK
    for home, (r, o) in enumerate(((r0, o0), (r1, o1), (r2, o2), (r3, o3))):
        named = r[:, width : width + LANES].astype(F32).astype(jnp.int32) - y * blocks
        mine = scores[home * full : (home + 1) * full]
        for c in range(CANDS):
            column = named[:, c : c + 1]
            picked = jnp.zeros((full, BLOCK), F32)
            for b in range(blocks):
                picked = jnp.where(column == b, mine[:, b * BLOCK : (b + 1) * BLOCK], picked)
            o[c * full : (c + 1) * full, :] = picked.astype(BF16)


def score_rows(place, gathered, impact):
    full = gathered[0].shape[0]
    one = jax.ShapeDtypeStruct((full * CANDS, BLOCK), BF16)
    vmem = pl.BlockSpec(memory_space=pltpu.VMEM)
    return pl.pallas_call(
        rows_kernel,
        out_shape=[one] * NY,
        in_specs=[pl.BlockSpec(memory_space=pltpu.SMEM)] + [vmem] * 5,
        out_specs=[vmem] * NY,
        compiler_params=pltpu.CompilerParams(vmem_limit_bytes=8 << 20),
        cost_estimate=pl.CostEstimate(flops=2 * 10**9, transcendentals=0, bytes_accessed=4 << 20),
        name="score_rows",
    )(place, *gathered, impact)


def score_kernel(pos_ref, impact_ref, dense_ref, *refs, extra, steps):
    piece_refs = refs[:6]
    extra_refs = refs[6:10] if extra else ()
    out_refs = refs[-NZ - 3 : -3]
    made_ref, own_ref, own_sem = refs[-3:]
    x, z, core = pos_ref[0], pos_ref[1], pos_ref[2]
    depth, share = piece_refs[0].shape
    chunk = made_ref.shape[1]
    rows = chunk // steps
    half = LANES // 2
    copies = []
    for i in range(2):
        at = (pl.ds((core ^ i) * depth, depth), pl.ds(x * share, share))
        copies.append(pltpu.make_async_copy(impact_ref.at[at], own_ref.at[i], own_sem.at[i]))
        copies[i].start()
    left = lax.broadcasted_iota(jnp.int32, (rows, LANES), 1) < half
    for step in range(steps):
        made = [None, None]
        for i in (2, 3, 4, 5, 6, 7, 0, 1):
            if step == 0 and i == 0:
                for copy in copies:
                    copy.wait()
            piece = own_ref[i] if i < 2 else piece_refs[i - 2][...]
            for part in range(2):
                first = part * chunk + step * rows
                block = dense_ref[first : first + rows, i * depth : (i + 1) * depth]
                one = jnp.dot(block, piece, preferred_element_type=F32)
                made[part] = one if made[part] is None else made[part] + one
        for m in range(NZ // 2):
            a = made[0][:, m * LANES : (m + 1) * LANES]
            b = made[1][:, m * LANES : (m + 1) * LANES]
            at = slice(step * rows, (step + 1) * rows)
            made_ref[2 * m, at, :] = jnp.where(left, a, pltpu.roll(b, half, 1)).astype(BF16)
            made_ref[2 * m + 1, at, :] = jnp.where(left, pltpu.roll(a, half, 1), b).astype(BF16)
    for j, out_ref in enumerate(out_refs):
        out_ref[:chunk, :] = made_ref[(z + j) & (NZ - 1)]
    if extra:
        pack_rows(z, chunk, extra_refs, out_refs)


def pack_rows(z, chunk, extra_refs, out_refs):
    total = extra_refs[0][...].astype(F32)
    for r in extra_refs[1:]:
        total = total + r[...].astype(F32)
    wide, own = LANES // NX, LANES // (NX * NZ)
    deep = total.shape[0] // NZ
    place = (lax.broadcasted_iota(jnp.int32, (deep, LANES), 1) & (wide - 1)) // own
    for j, out_ref in enumerate(out_refs):
        to_z = (z + j) & (NZ - 1)
        packed = jnp.zeros((deep, LANES), F32)
        for g in range(NZ):
            part = total[g * deep : (g + 1) * deep]
            part = pltpu.roll(part, ((g - to_z) * own) & (LANES - 1), 1)
            packed = jnp.where(place == g, part, packed)
        out_ref[chunk:, :] = jnp.concatenate([packed, jnp.zeros_like(packed)], axis=0).astype(BF16)


def score_chunk(place, impact, dense, pieces, sums):
    chunk = dense.shape[0] // 2
    width = dense.shape[1]
    depth, share = pieces[0].shape
    extra = sums is not None
    out_rows = chunk + (2 * sums[0].shape[0] // NZ if extra else 0)
    more = tuple(sums) if extra else ()
    vmem = pl.BlockSpec(memory_space=pltpu.VMEM)
    hbm = pl.BlockSpec(memory_space=pltpu.HBM)
    return pl.pallas_call(
        functools.partial(score_kernel, extra=extra, steps=1),
        out_shape=[jax.ShapeDtypeStruct((out_rows, LANES), BF16)] * NZ,
        in_specs=[pl.BlockSpec(memory_space=pltpu.SMEM), hbm] + [vmem] * (1 + len(pieces) + len(more)),
        out_specs=[vmem] * NZ,
        scratch_shapes=[
            pltpu.VMEM((NZ, chunk, LANES), BF16),
            pltpu.VMEM((2, depth, share), BF16),
            pltpu.SemaphoreType.DMA((2,)),
        ],
        compiler_params=pltpu.CompilerParams(vmem_limit_bytes=12 << 20),
        cost_estimate=pl.CostEstimate(
            flops=2 * chunk * width * share * 2, transcendentals=0, bytes_accessed=chunk * width * 4
        ),
        name="score_chunk",
    )(place, kept_in_hbm(impact), dense, *pieces, *more)


def cut_kernel(pos_ref, impact_ref, query_ref, named_ref, ids_ref, weights_ref, *refs, shifts):
    rows_ref, ids_here, weights_here = refs[:3]
    out_refs, named_here, sem = refs[3:-2], refs[-2], refs[-1]
    x, core = pos_ref[0], pos_ref[2]
    full, width = query_ref.shape
    count = len(out_refs) * CUTS
    copies = [
        pltpu.make_async_copy(named_ref, named_here, sem.at[count]),
        pltpu.make_async_copy(query_ref, rows_ref.at[:, pl.ds(0, width)], sem.at[count + 1]),
        pltpu.make_async_copy(ids_ref, ids_here, sem.at[count + 2]),
        pltpu.make_async_copy(weights_ref, weights_here, sem.at[count + 3]),
    ]
    for i, (out_ref, r) in enumerate(zip(out_refs, shifts)):
        depth, share = out_ref.shape
        part = depth // CUTS
        to_x = (x - r) & (NX - 1)
        for j in range(CUTS):
            at = (pl.ds(core * depth + j * part, part), pl.ds(to_x * share, share))
            copies.append(
                pltpu.make_async_copy(impact_ref.at[at], out_ref.at[pl.ds(j * part, part)], sem.at[i * CUTS + j])
            )
    for copy in copies:
        copy.start()
    copies[0].wait()
    named = named_here[...].astype(F32)
    named = jnp.concatenate([named, jnp.zeros((LANES - CANDS, full), F32)], axis=0)
    rows_ref[:, width:] = named.T.astype(BF16)
    for copy in copies[1:]:
        copy.wait()


def cut_slices(place, impact, query_rows, candidates, ids, weights, shifts):
    full, width = query_rows.shape
    one = jax.ShapeDtypeStruct((impact.shape[0] // 2, impact.shape[1] // NX), BF16)
    vmem = pl.BlockSpec(memory_space=pltpu.VMEM)
    hbm = pl.BlockSpec(memory_space=pltpu.HBM)
    rows, ids_here, weights_here, *cuts = pl.pallas_call(
        functools.partial(cut_kernel, shifts=shifts),
        out_shape=[
            jax.ShapeDtypeStruct((full, width + LANES), BF16),
            jax.ShapeDtypeStruct(ids.shape, ids.dtype),
            jax.ShapeDtypeStruct(weights.shape, weights.dtype),
        ]
        + [one] * len(shifts),
        in_specs=[pl.BlockSpec(memory_space=pltpu.SMEM)] + [hbm] * 5,
        out_specs=[vmem] * (3 + len(shifts)),
        scratch_shapes=[
            pltpu.VMEM((CANDS, full), jnp.int32),
            pltpu.SemaphoreType.DMA((len(shifts) * CUTS + 4,)),
        ],
        compiler_params=pltpu.CompilerParams(vmem_limit_bytes=4 << 20),
        name="cut_slices",
    )(place, *[kept_in_hbm(a) for a in (impact, query_rows, candidates.T, ids, weights)])
    return rows, ids_here, weights_here, cuts


def summed_chunk(parts, to_ref, column):
    half = LANES // 2
    chunk = to_ref.shape[1] // 2 if column is None else to_ref.shape[1] // 4
    column = column or 0
    total = parts[0][:chunk].astype(F32)
    for part in parts[1:]:
        total = total + part[:chunk].astype(F32)
    turned = total.T.astype(BF16)
    to_ref[:, column : column + chunk] = turned[:half]
    to_ref[:, column + chunk : column + 2 * chunk] = turned[half:]


def half_kernel(a0, a1, a2, done_ref):
    summed_chunk((a0, a1, a2), done_ref, None)


def finish_half(parts):
    chunk = parts[0].shape[0]
    vmem = pl.BlockSpec(memory_space=pltpu.VMEM)
    return pl.pallas_call(
        half_kernel,
        out_shape=jax.ShapeDtypeStruct((LANES // 2, 2 * chunk), BF16),
        in_specs=[vmem] * 3,
        out_specs=vmem,
        compiler_params=pltpu.CompilerParams(vmem_limit_bytes=4 << 20),
        name="finish_half",
    )(*parts)


def final_kernel(pos_ref, done_ref, b0, b1, b2, first_ref, rescored_ref):
    x = pos_ref[0]
    columns = done_ref.shape[1]
    first_ref[:, :columns] = done_ref[...]
    summed_chunk((b0, b1, b2), first_ref, columns)
    chunk = columns // 2
    more = b0[chunk:].astype(F32) + b1[chunk:].astype(F32) + b2[chunk:].astype(F32)
    share = LANES // (NX * NZ)
    deep = more.shape[0] // 2
    turned = pltpu.roll(more, (LANES - x * (LANES // NX)) & (LANES - 1), 1).T
    for g in range(NZ):
        part = turned[g * share : (g + 1) * share, :deep]
        rescored_ref[g // 2, :, (g % 2) * deep : (g % 2 + 1) * deep] = part


def finish(place, done, parts, full):
    vmem = pl.BlockSpec(memory_space=pltpu.VMEM)
    return pl.pallas_call(
        final_kernel,
        out_shape=[
            jax.ShapeDtypeStruct((LANES // 2, 2 * done.shape[1]), BF16),
            jax.ShapeDtypeStruct((CANDS, LANES // (NX * NZ), full), F32),
        ],
        in_specs=[pl.BlockSpec(memory_space=pltpu.SMEM)] + [vmem] * 4,
        out_specs=[vmem] * 2,
        compiler_params=pltpu.CompilerParams(vmem_limit_bytes=8 << 20),
        name="finish",
    )(place, done, *parts)


def added(*parts):
    total = parts[0].astype(F32)
    for part in parts[1:]:
        total = total + part.astype(F32)
    return total.astype(BF16)


def after(values, done):
    return lax.optimization_barrier((values, done))[0]


def sent(values):
    out = {}
    for way in (1, -1):
        out[way] = shifted(values[way], "z", way)
    return out


def first_step(made, long_way):
    ahead = shifted(made[4], "z", 2 * long_way)
    return ahead, sent({1: made[3], -1: made[5]})


def second_values(made, long_way, ahead, carried):
    values = {1: [carried[1], made[2]], -1: [carried[-1], made[6]]}
    values[long_way].append(ahead)
    return {way: added(*parts) for way, parts in values.items()}


def third_values(made, carried):
    return {1: added(carried[1], made[1]), -1: added(carried[-1], made[7])}


def rings(made_a, made_b, start_a, start_b):
    (ahead_a, going_a), (ahead_b, going_b) = start_a, start_b
    going_a = sent(second_values(made_a, 1, ahead_a, going_a))
    going_b = sent(second_values(made_b, -1, ahead_b, going_b))
    going_a = sent(third_values(made_a, going_a))
    going_b = sent(third_values(made_b, going_b))
    return (going_a[1], going_a[-1]), (going_b[1], going_b[-1])


def scored(term_ids, term_weights, impact, query_rows, candidates):
    x = lax.axis_index("x")
    z = lax.axis_index("z")
    y = lax.axis_index("prange")
    core = lax.axis_index("query")
    place = jnp.stack([x, z, core, y]).astype(jnp.int32)
    shard_width = impact.shape[0]
    full = query_rows.shape[0]

    shifts = (1, 3, 2)
    rows, ids, weights, cuts = cut_slices(place, impact, query_rows, candidates, term_ids.T, term_weights.T, shifts)
    near = {}
    for r, one in zip(shifts, cuts):
        near[r] = shifted(one, "x", -r)
    gathered = [rows]
    for r in (1, 2, 3):
        gathered.append(shifted(rows, "prange", -r))
    dense_a = build_dense(place, ids, weights, NX * shard_width, 0)
    gathered = after(gathered, dense_a)
    by_home = score_rows(place, gathered, impact)
    back = [by_home[0]]
    for r in (1, 2, 3):
        back.append(shifted(by_home[r], "prange", r))
    ids = after(ids, by_home)
    dense_b = build_dense(place, ids, weights, NX * shard_width, 1)

    pieces = {}
    for r in (1, 3, 2):
        ready = after(near[r], dense_b)
        pieces[r] = [ready, shifted(ready, "query", 1)]
    mine = added(*after(back, dense_b))
    sums = [mine]
    for r in (1, 2, 3):
        sums.append(shifted(mine, "x", r))
    pieces = pieces[1] + pieces[2] + pieces[3]
    made_a = score_chunk(place, impact, dense_a, pieces, None)
    start_a = first_step(made_a, 1)
    made_b = score_chunk(place, impact, dense_b, pieces, sums)
    start_b = first_step(made_b, -1)
    (a1, a2), (b1, b2) = rings(made_a, made_b, start_a, start_b)
    done = finish_half((made_a[0], a1, a2))
    first, rescored = finish(place, done, (made_b[0], b1, b2), full)
    return (first[None], jnp.transpose(rescored, (2, 0, 1)))


def solution(mesh):
    finer = Mesh(
        mesh.devices.reshape(NX, NZ, mesh.shape["prange"], mesh.shape["query"]),
        ("x", "z", "prange", "query"),
    )
    vocab = ("x", "z")
    in_specs = (
        P("query", None),
        P("query", None),
        P(vocab, "prange"),
        P(("prange", "query"), vocab),
        P(("prange", "query"), None),
    )
    out_specs = (P("prange", vocab, "query"), P(("prange", "query"), None, vocab))
    return jax.shard_map(scored, mesh=finer, in_specs=in_specs, out_specs=out_specs, check_vma=False)
```
